256 devices in a mesh: state: 4 (over y_lo, core), walker: 64 (over x, y_hi, z).
Axes of the slice: x: 4, y: 4 (y_hi: 2, y_lo: 2; y = y_hi * 2 + y_lo), z: 8, core: 2. Of those that a mesh axis runs over, the one named last changes fastest.
Arguments:
- walkers: float32 [8, 64, 126], P('state', 'walker'), may hold values from -8 to 8
- nuclei: float32 [12, 3], replicated, may hold values from -5 to 5
- w_embed: float32 [8, 48, 256], P('state'), may hold values from -0.875 to 0.875
- w_query: float32 [8, 1, 256, 256], P('state'), may hold values from -16 to 16
- w_key: float32 [8, 1, 256, 256], P('state'), may hold values from -0.375 to 0.375
- w_value: float32 [8, 1, 256, 256], P('state'), may hold values from -0.375 to 0.375
- w_attn_out: float32 [8, 1, 256, 256], P('state'), may hold values from -0.375 to 0.375
- w_mlp: float32 [8, 1, 256, 256], P('state'), may hold values from -0.375 to 0.375
- b_mlp: float32 [8, 1, 256], P('state'), may hold values from -3 to 3
- w_out: float32 [8, 256], P('state'), may hold values from -0.375 to 0.375
Outputs:
- margins: float32 [8, 8], replicated
- grad_embed: float32 [8, 48, 256], P('state')
- grad_query: float32 [8, 1, 256, 256], P('state')
- grad_key: float32 [8, 1, 256, 256], P('state')
- grad_value: float32 [8, 1, 256, 256], P('state')
- grad_attn_out: float32 [8, 1, 256, 256], P('state')
- grad_mlp: float32 [8, 1, 256, 256], P('state')
- grad_bias: float32 [8, 1, 256], P('state')
- grad_out: float32 [8, 256], P('state')
The draws below stay inside these ranges and needn't reach their ends.
All inputs are finite; a program needn't handle non-finite values.
Results may differ from the reference program's by a relative error of at most 0.0003.
Values sent between devices are 32-bit elements; how exact they have to be, the bound alone decides.
No kernel may reach another device: no remote copies, remote signals or barrier semaphores. Data moves between devices by JAX's collectives and lax.ppermute only.
A program may use at most 64 MiB of HBM per device.

```python
import math
import jax
import jax.numpy as jnp
from jax import lax

D = 256
HEADS = 4
NE = 42
NA = 12
FEAT = 48
LAYERS = 1
NSTATES = 8
WALKERS = 64


def draw_w_query(key, part):
    base = jax.random.truncated_normal(key, -4.0, 4.0, (NSTATES, LAYERS, D, D), jnp.float32)
    return base * (16.0 / D)


def block_levels(rng, shape, shards, least, largest):
    loudness = 1.0
    for dim, blocks in shards:
        draws = jax.random.uniform(jax.random.fold_in(jax.random.fold_in(rng, 6), dim), (blocks,), jnp.float32, least / len(shards), largest / len(shards))
        loudness = loudness * jnp.repeat(jnp.exp(draws), shape[dim] // blocks).reshape((-1,) + (1,) * (len(shape) - 1 - dim))
    return loudness


def scatter_about(own_key, extent, deviation, limit, split=(), kind=jnp.bfloat16):
    entries = jax.random.normal(own_key, extent, jnp.float32) * deviation
    if len(split) > 0:
        entries = block_levels(own_key, extent, split, -0.22, 0.18) * entries
    return jnp.clip(entries, min=-limit, max=limit).astype(kind)


def setup_inputs(seed: int = 0) -> dict:
    key_list = jax.random.split(jax.random.key(seed), 11)
    return {
        "walkers": scatter_about(key_list[0], (NSTATES, WALKERS, 3 * NE), 1.5, 8.0, ((0, 4), (1, 64)), jnp.float32),
        "nuclei": scatter_about(key_list[1], (NA, 3), 1.3, 5.0, (), jnp.float32),
        "w_embed": scatter_about(key_list[2], (NSTATES, FEAT, D), FEAT ** -0.5, 0.875, ((0, 4),), jnp.float32),
        "w_query": draw_w_query(jax.random.fold_in(key_list[10], 71), 0),
        "w_key": scatter_about(key_list[4], (NSTATES, LAYERS, D, D), D ** -0.5, 0.375, ((0, 4),), jnp.float32),
        "w_value": scatter_about(key_list[5], (NSTATES, LAYERS, D, D), D ** -0.5, 0.375, ((0, 4),), jnp.float32),
        "w_attn_out": scatter_about(key_list[6], (NSTATES, LAYERS, D, D), D ** -0.5, 0.375, ((0, 4),), jnp.float32),
        "w_mlp": scatter_about(key_list[7], (NSTATES, LAYERS, D, D), D ** -0.5, 0.375, ((0, 4),), jnp.float32),
        "b_mlp": scatter_about(key_list[8], (NSTATES, LAYERS, D), 0.5, 3.0, ((0, 4),), jnp.float32),
        "w_out": scatter_about(key_list[9], (NSTATES, D), D ** -0.5, 0.375, ((0, 4),), jnp.float32),
    }


highest = lax.Precision.HIGHEST
eps = 1e-05

def layer_norm(hidden):
    centre = hidden - lax.optimization_barrier(jnp.mean(hidden, axis=-1, keepdims=True))
    spread = lax.optimization_barrier(jnp.mean(centre * centre, axis=-1, keepdims=True))
    return centre / jnp.sqrt(spread + eps)

def electron_features(positions, nuclei):
    batch_size = positions.shape[0]
    electrons = positions.reshape(batch_size, -1, 1, 3)
    offset = electrons - nuclei[None, None, :, :]
    distance = jnp.sqrt(lax.optimization_barrier(jnp.sum(offset * offset, axis=-1, keepdims=True)) + 1.0)
    joined = jnp.concatenate([offset, distance], axis=-1)
    return joined.reshape(batch_size, electrons.shape[1], -1)

def network(parameters, electron_feats):
    w_embed, w_query, w_key, w_value, w_attn_out, w_mlp, b_mlp, w_out = parameters
    batch_size, electron_count = (electron_feats.shape[0], electron_feats.shape[1])
    width = w_embed.shape[1]
    head_size = width // HEADS
    hidden = jnp.einsum('bef,fd->bed', electron_feats, w_embed, precision=highest)
    for layer_index in range(w_query.shape[0]):
        normed = layer_norm(hidden)
        queries = jnp.einsum('bed,dc->bec', normed, w_query[layer_index], precision=highest).reshape(batch_size, electron_count, HEADS, head_size)
        key_heads = jnp.einsum('bed,dc->bec', normed, w_key[layer_index], precision=highest).reshape(batch_size, electron_count, HEADS, head_size)
        value_heads = jnp.einsum('bed,dc->bec', normed, w_value[layer_index], precision=highest).reshape(batch_size, electron_count, HEADS, head_size)
        scores = jnp.einsum('behc,bfhc->bhef', queries, key_heads, precision=highest) / math.sqrt(head_size)
        row_max = lax.stop_gradient(lax.optimization_barrier(jnp.max(scores, axis=-1, keepdims=True)))
        weights = jnp.exp(scores - row_max)
        attention = weights / lax.optimization_barrier(jnp.sum(weights, axis=-1, keepdims=True))
        mixed = jnp.einsum('bhef,bfhc->behc', attention, value_heads, precision=highest).reshape(batch_size, electron_count, width)
        hidden = hidden + jnp.einsum('bed,dc->bec', mixed, w_attn_out[layer_index], precision=highest)
        inner = jnp.einsum('bed,dc->bec', layer_norm(hidden), w_mlp[layer_index], precision=highest)
        hidden = hidden + jnp.tanh(inner + b_mlp[layer_index])
    return jnp.einsum('bed,d->b', hidden, w_out, precision=highest) / electron_count

def reference(walkers, nuclei, w_embed, w_query, w_key, w_value, w_attn_out, w_mlp, b_mlp, w_out):
    state_total, walker_count = (walkers.shape[0], walkers.shape[1])
    parameters = (w_embed, w_query, w_key, w_value, w_attn_out, w_mlp, b_mlp, w_out)
    electron_feats = electron_features(walkers.reshape(state_total * walker_count, -1), nuclei)
    log_amplitude = lax.map(lambda net_params: network(net_params, electron_feats), parameters)
    log_amplitude = log_amplitude.reshape(state_total, state_total, walker_count)
    home_logs = jnp.diagonal(log_amplitude, axis1=0, axis2=1).T
    ratios = jnp.exp(log_amplitude - home_logs[None])
    margins = lax.optimization_barrier(jnp.mean(ratios, axis=2)).T
    identity = jnp.eye(state_total, dtype=jnp.float32)
    coupling = margins.T * (1.0 - identity)
    denominator = jnp.einsum('ij,jix->ix', coupling, ratios, precision=highest) / walker_count
    cotangent = coupling.T[:, :, None] * ratios / walker_count - identity[:, :, None] * denominator[None]

    def pull_back(inputs):
        net_params, net_cotangent = inputs
        _, pullback = jax.vjp(lambda chosen: network(chosen, electron_feats), net_params)
        return pullback(net_cotangent)[0]
    gradients = lax.map(pull_back, (parameters, cotangent.reshape(state_total, -1)))
    return (margins, gradients[0], gradients[1], gradients[2], gradients[3], gradients[4], gradients[5], gradients[6], gradients[7])
```

```python
import jax
import jax.numpy as jnp
from jax import lax
from jax.experimental import pallas as pl
from jax.experimental.pallas import tpu as pltpu
from jax.sharding import Mesh, PartitionSpec as P

HEADS = 4
NE = 42
ROWS = 48
D = 256
FEAT = 48
EPS = 1e-05
HIGHEST = lax.Precision.HIGHEST
NN = (((1,), (0,)), ((), ()))
NT = (((1,), (1,)), ((), ()))
TN = (((0,), (0,)), ((), ()))


def exact(a, b, dims):
    return lax.dot_general(a, b, dims, precision=HIGHEST, preferred_element_type=jnp.float32)


def halves(a):
    high = a.astype(jnp.bfloat16)
    return high, (a - high.astype(jnp.float32)).astype(jnp.bfloat16)


def three(a, b, dims):
    def one(x, y):
        return lax.dot_general(x, y, dims, preferred_element_type=jnp.float32)

    return one(a[0], b[0]) + (one(a[0], b[1]) + one(a[1], b[0]))


def normalise(hidden):
    centre = hidden - jnp.mean(hidden, axis=-1, keepdims=True)
    scale = lax.rsqrt(jnp.mean(centre * centre, axis=-1, keepdims=True) + EPS)
    return centre * scale, scale


def normalise_back(grad, normed, scale):
    return scale * (
        grad
        - jnp.mean(grad, axis=-1, keepdims=True)
        - normed * jnp.mean(grad * normed, axis=-1, keepdims=True)
    )


def head_masks():
    lane = lax.broadcasted_iota(jnp.int32, (1, D), 1)
    return [(lane // (D // HEADS)) == h for h in range(HEADS)]


def spread(block, masks):
    return jnp.concatenate([jnp.where(m, block, 0.0) for m in masks], axis=0)


def gather_heads(stacked, masks):
    out = jnp.where(masks[0], stacked[:ROWS], 0.0)
    for h in range(1, HEADS):
        out = out + jnp.where(masks[h], stacked[h * ROWS : (h + 1) * ROWS], 0.0)
    return out


def forward_kernel(
    walk_ref, nuc_ref, we_ref, wq_ref, wk_ref, wv_ref, wo_ref, wm_ref, b_ref, wout_ref,
    la_ref, feat_ref, x_ref, r1_ref, q_ref, k_ref, v_ref, at_ref, mix_ref, y_ref, r2_ref, t_ref, h2_ref,
    pos_ref,
):
    count = walk_ref.shape[0]
    width = walk_ref.shape[1]
    electron = lax.broadcasted_iota(jnp.int32, (ROWS, width), 0)
    lane = lax.broadcasted_iota(jnp.int32, (ROWS, width), 1)
    picks = [lane == 3 * electron + c for c in range(3)]
    flane = lax.broadcasted_iota(jnp.int32, (1, FEAT), 1)
    kind = flane % 4
    masks = head_masks()
    n = [nuc_ref[c : c + 1, :] for c in range(3)]
    for w in range(count):
        row = jnp.broadcast_to(walk_ref[w : w + 1, :], (ROWS, width))
        off = [
            jnp.sum(jnp.where(picks[c], row, 0.0), axis=1, keepdims=True) - n[c] for c in range(3)
        ]
        dist = jnp.sqrt(off[0] * off[0] + off[1] * off[1] + off[2] * off[2] + 1.0)
        feat = jnp.where(kind == 0, off[0], jnp.where(kind == 1, off[1], jnp.where(kind == 2, off[2], dist)))
        feat_ref[w * ROWS : (w + 1) * ROWS, :] = feat
    h0 = exact(feat_ref[...], we_ref[0], NN)
    x, r1 = normalise(h0)
    x_ref[...] = x
    r1_ref[...] = r1
    q_ref[...] = exact(x, wq_ref[0], NN) * 0.125
    k_ref[...] = exact(x, wk_ref[0], NN)
    v_ref[...] = three(halves(x), halves(wv_ref[0]), NN)
    key_row = lax.broadcasted_iota(jnp.int32, (ROWS, HEADS * ROWS), 0)

    def attend(w, carry):
        rows = pl.ds(pl.multiple_of(w * ROWS, ROWS), ROWS)
        scores = exact(k_ref[rows, :], spread(q_ref[rows, :], masks), NT)
        scores = jnp.where(key_row < NE, scores, -1e30)
        weights = jnp.exp(scores - jnp.max(scores, axis=0, keepdims=True))
        attention = weights / jnp.sum(weights, axis=0, keepdims=True)
        at_ref[rows, :] = attention
        mixed = three(halves(attention), halves(v_ref[rows, :]), TN)
        mix_ref[rows, :] = gather_heads(mixed, masks)
        return carry

    lax.fori_loop(0, count, attend, 0)
    h1 = h0 + three(halves(mix_ref[...]), halves(wo_ref[0]), NN)
    y, r2 = normalise(h1)
    y_ref[...] = y
    r2_ref[...] = r2
    t = jnp.tanh(three(halves(y), halves(wm_ref[0]), NN) + b_ref[0])
    t_ref[...] = t
    h2 = h1 + t
    real = lax.broadcasted_iota(jnp.int32, (ROWS, 1), 0) < NE
    for w in range(count):
        total = jnp.sum(jnp.where(real, h2[w * ROWS : (w + 1) * ROWS, :], 0.0), axis=0, keepdims=True) / NE
        h2_ref[w : w + 1, :] = total
        la_ref[w : w + 1, :] = jnp.broadcast_to(
            jnp.sum(total * wout_ref[0], axis=1, keepdims=True), (1, 128)
        )


def backward_kernel(
    r1_ref, x_ref, q_ref, k_ref, v_ref, at_ref, y_ref, r2_ref, t_ref,
    wq_ref, wk_ref, wv_ref, wo_ref, wm_ref, wout_ref,
    dm_ref, dh1_ref, dqkv_ref, dh0_ref,
    do_ref,
):
    total = x_ref.shape[0]
    count = total // ROWS
    masks = head_masks()
    row = lax.broadcasted_iota(jnp.int32, (total, 1), 0)
    real = (row % ROWS) < NE
    g = jnp.where(real, wout_ref[0] / NE, 0.0)
    t = t_ref[...]
    dm = g * (1.0 - t * t)
    dm_ref[...] = dm
    dy = three(halves(dm), halves(wm_ref[0]), NT)
    dh1 = g + normalise_back(dy, y_ref[...], r2_ref[...])
    dh1_ref[...] = dh1
    do_ref[...] = three(halves(dh1), halves(wo_ref[0]), NT)

    def attend(w, carry):
        rows = pl.ds(pl.multiple_of(w * ROWS, ROWS), ROWS)
        attention = at_ref[rows, :]
        do = halves(spread(do_ref[rows, :], masks))
        da = three(halves(v_ref[rows, :]), do, NT)
        dqkv_ref[rows, 2 * D :] = three(halves(attention), do, NN)
        ds = attention * (da - jnp.sum(da * attention, axis=0, keepdims=True))
        ds = halves(ds)
        dqkv_ref[rows, D : 2 * D] = three(ds, halves(spread(q_ref[rows, :], masks)), NN)
        dqkv_ref[rows, :D] = gather_heads(three(ds, halves(k_ref[rows, :]), TN), masks) * 0.125
        return carry

    lax.fori_loop(0, count, attend, 0)
    dx = three(halves(dqkv_ref[:, :D]), halves(wq_ref[0]), NT)
    dx = dx + three(halves(dqkv_ref[:, D : 2 * D]), halves(wk_ref[0]), NT)
    dx = dx + three(halves(dqkv_ref[:, 2 * D :]), halves(wv_ref[0]), NT)
    dh0_ref[...] = dh1 + normalise_back(dx, x_ref[...], r1_ref[...])


def weights_kernel(c_ref, feat_ref, x_ref, mix_ref, y_ref, h2_ref, dm_ref, dh1_ref, dqkv_ref, dh0_ref, out_ref):
    count = c_ref.shape[0]
    total = x_ref.shape[0]
    factor = jnp.concatenate(
        [jnp.broadcast_to(c_ref[w : w + 1, :1], (ROWS, 1)) for w in range(count)], axis=0
    )
    dm = factor * dm_ref[...]
    out_ref[0:D, :] = three(halves(y_ref[...]), halves(dm), TN)
    out_ref[D : 2 * D, :] = three(halves(mix_ref[...]), halves(factor * dh1_ref[...]), TN)
    x = halves(x_ref[...])
    for i in range(3):
        out_ref[(2 + i) * D : (3 + i) * D, :] = three(x, halves(factor * dqkv_ref[:, i * D : (i + 1) * D]), TN)
    base = 5 * D
    out_ref[base : base + FEAT, :] = three(halves(feat_ref[...]), halves(factor * dh0_ref[...]), TN)
    base = base + FEAT
    out_ref[base : base + 1, :] = jnp.sum(dm, axis=0, keepdims=True)
    out_ref[base + 1 : base + 2, :] = jnp.sum(c_ref[:, :1] * h2_ref[...], axis=0, keepdims=True)
    out_ref[base + 2 :, :] = jnp.zeros((out_ref.shape[0] - base - 2, D), jnp.float32)


OUT_ROWS = 1344


def vmem():
    return pl.BlockSpec(memory_space=pltpu.VMEM)


def shape(*s):
    return jax.ShapeDtypeStruct(s, jnp.float32)


def offsets(n):
    return [n // 2] + [d for k in range(1, n // 2) for d in (k, -k)] if n > 2 else [1]


def shift(v, axis, d, n):
    return lax.ppermute(v, axis, [(i, (i + d) % n) for i in range(n)])


def gather(v, axis, n):
    me = lax.axis_index(axis)
    out = jnp.zeros((n,) + v.shape, v.dtype)
    out = lax.dynamic_update_index_in_dim(out, v, me, 0)
    for d in offsets(n):
        out = lax.dynamic_update_index_in_dim(out, shift(v, axis, d, n), (me - d) % n, 0)
    return out


def scatter_sum(v, axis, n):
    me = lax.axis_index(axis)
    blocks = v.reshape((n, v.shape[0] // n) + v.shape[1:])
    total = lax.dynamic_index_in_dim(blocks, me, 0, False)
    for d in offsets(n):
        total = total + shift(lax.dynamic_index_in_dim(blocks, (me + d) % n, 0, False), axis, d, n)
    return total


def shards(walkers, nuclei, w_embed, w_query, w_key, w_value, w_attn_out, w_mlp, b_mlp, w_out):
    nx, ny, nz = lax.axis_size("x"), lax.axis_size("yh"), lax.axis_size("z")
    groups = lax.axis_size("ylo") * lax.axis_size("core")
    walker_count = nx * ny * nz
    yh = lax.axis_index("yh")
    state = lax.axis_index("ylo") * lax.axis_size("core") + lax.axis_index("core")
    states = 2 * groups
    net = state * 2 + yh
    near = ("ylo", "core", "yh")
    gathered = lax.all_gather(walkers.reshape(2, 126), near, axis=0, tiled=False)
    walk = gathered.reshape(groups, ny, 2, 126).transpose(0, 2, 1, 3).reshape(states * ny, 126)
    nuc = jnp.repeat(nuclei.T, 4, axis=1)

    def pick(a):
        return lax.dynamic_slice_in_dim(a, yh, 1, 0)

    we = pick(w_embed)
    wq, wk, wv, wo, wm = [pick(a[:, 0]) for a in (w_query, w_key, w_value, w_attn_out, w_mlp)]
    b, wout = pick(b_mlp), pick(w_out[:, None, :])
    count = states * ny
    total = count * ROWS
    grant = pltpu.CompilerParams(vmem_limit_bytes=60 * 1024 * 1024)
    la, feat, x, r1, q, k, v, at, mix, y, r2, t, h2 = pl.pallas_call(
        forward_kernel,
        out_shape=[shape(count, 128), shape(total, FEAT), shape(total, D), shape(total, 1), shape(total, D),
                   shape(total, D), shape(total, D), shape(total, HEADS * ROWS), shape(total, D),
                   shape(total, D), shape(total, 1), shape(total, D), shape(count, D)],
        in_specs=[vmem()] * 10,
        out_specs=[vmem()] * 13,
        scratch_shapes=[pltpu.VMEM((8, 128), jnp.float32)],
        compiler_params=grant,
    )(walk, nuc, we, wq, wk, wv, wo, wm, b, wout)
    dm, dh1, dqkv, dh0 = pl.pallas_call(
        backward_kernel,
        out_shape=[shape(total, D), shape(total, D), shape(total, 3 * D), shape(total, D)],
        in_specs=[vmem()] * 15,
        out_specs=[vmem()] * 4,
        scratch_shapes=[pltpu.VMEM((total, D), jnp.float32)],
        compiler_params=grant,
    )(r1, x, q, k, v, at, y, r2, t, wq, wk, wv, wo, wm, wout)

    logs = lax.all_gather(la[:, 0], near, axis=0, tiled=False)
    logs = logs.reshape(groups, ny, states, ny)
    logs = logs.reshape(states, states, ny)
    home = jnp.diagonal(logs, axis1=0, axis2=1).T
    ratios = jnp.exp(logs - home[None])
    part = jnp.sum(ratios, axis=2).T
    sums = jnp.sum(gather(jnp.sum(gather(part, "x", nx), axis=0), "z", nz), axis=0)
    margins = sums / walker_count
    identity = jnp.eye(states, dtype=jnp.float32)
    coupling = margins.T * (1.0 - identity)
    denominator = jnp.sum(coupling[:, :, None] * ratios.transpose(1, 0, 2), axis=1) / walker_count
    cot = coupling.T[:, :, None] * ratios / walker_count - identity[:, :, None] * denominator[None]
    own = lax.dynamic_index_in_dim(cot, net, 0, False).reshape(count)
    own = jnp.broadcast_to(own[:, None], (count, 128))

    partial = pl.pallas_call(
        weights_kernel,
        out_shape=shape(OUT_ROWS, D),
        in_specs=[vmem()] * 10,
        out_specs=vmem(),
        compiler_params=grant,
    )(own, feat, x, mix, y, h2, dm, dh1, dqkv, dh0)
    mine = scatter_sum(scatter_sum(partial, "x", nx), "z", nz)
    both = gather(mine, "yh", ny)
    both = gather(both, "z", nz)
    both = gather(both, "x", nx)
    full = both.transpose(2, 0, 1, 3, 4).reshape(ny, OUT_ROWS, D)
    base = 5 * D
    return (
        margins,
        full[:, base : base + FEAT],
        full[:, 2 * D : 3 * D][:, None],
        full[:, 3 * D : 4 * D][:, None],
        full[:, 4 * D : 5 * D][:, None],
        full[:, D : 2 * D][:, None],
        full[:, :D][:, None],
        full[:, base + FEAT : base + FEAT + 1],
        full[:, base + FEAT + 1],
    )


def solution(mesh):
    fine = Mesh(mesh.devices.reshape(2, 2, 4, 2, 8), ("ylo", "core", "x", "yh", "z"))
    s, w = ("ylo", "core"), ("x", "yh", "z")
    return jax.shard_map(
        shards,
        mesh=fine,
        in_specs=(P(s, w, None), P()) + (P(s),) * 8,
        out_specs=(P(),) + (P(s),) * 8,
        check_vma=False,
    )
```

```python
import jax
import jax.numpy as jnp
from jax import lax
from jax.experimental import pallas as pl
from jax.experimental.pallas import tpu as pltpu
from jax.sharding import Mesh, PartitionSpec as P

HEADS = 4
NE = 42
ROWS = 48
D = 256
FEAT = 48
EPS = 1e-05
HIGHEST = lax.Precision.HIGHEST
NN = (((1,), (0,)), ((), ()))
NT = (((1,), (1,)), ((), ()))
TN = (((0,), (0,)), ((), ()))


def exact(a, b, dims):
    return lax.dot_general(a, b, dims, precision=HIGHEST, preferred_element_type=jnp.float32)


def halves(a):
    high = a.astype(jnp.bfloat16)
    return high, (a - high.astype(jnp.float32)).astype(jnp.bfloat16)


def three(a, b, dims):
    def one(x, y):
        return lax.dot_general(x, y, dims, preferred_element_type=jnp.float32)

    return one(a[0], b[0]) + (one(a[0], b[1]) + one(a[1], b[0]))


def normalise(hidden):
    centre = hidden - jnp.mean(hidden, axis=-1, keepdims=True)
    scale = lax.rsqrt(jnp.mean(centre * centre, axis=-1, keepdims=True) + EPS)
    return centre * scale, scale


def normalise_back(grad, normed, scale):
    return scale * (
        grad
        - jnp.mean(grad, axis=-1, keepdims=True)
        - normed * jnp.mean(grad * normed, axis=-1, keepdims=True)
    )


def head_masks():
    lane = lax.broadcasted_iota(jnp.int32, (1, D), 1)
    return [(lane // (D // HEADS)) == h for h in range(HEADS)]


def spread(block, masks):
    return jnp.concatenate([jnp.where(m, block, 0.0) for m in masks], axis=0)


def gather_heads(stacked, masks):
    out = jnp.where(masks[0], stacked[:ROWS], 0.0)
    for h in range(1, HEADS):
        out = out + jnp.where(masks[h], stacked[h * ROWS : (h + 1) * ROWS], 0.0)
    return out


def forward_kernel(
    net_ref, walk_ref, nuc_ref, we_ref, wq_ref, wk_ref, wv_ref, wo_ref, wm_ref, b_ref, wout_ref,
    la_ref, feat_ref, x_ref, r1_ref, q_ref, k_ref, v_ref, at_ref, mix_ref, y_ref, r2_ref, t_ref, h2_ref,
):
    count = walk_ref.shape[0]
    width = walk_ref.shape[1]
    electron = lax.broadcasted_iota(jnp.int32, (ROWS, width), 0)
    lane = lax.broadcasted_iota(jnp.int32, (ROWS, width), 1)
    picks = [lane == 3 * electron + c for c in range(3)]
    flane = lax.broadcasted_iota(jnp.int32, (1, FEAT), 1)
    kind = flane % 4
    masks = head_masks()
    n = [nuc_ref[c : c + 1, :] for c in range(3)]
    for w in range(count):
        row = jnp.broadcast_to(walk_ref[w : w + 1, :], (ROWS, width))
        off = [
            jnp.sum(jnp.where(picks[c], row, 0.0), axis=1, keepdims=True) - n[c] for c in range(3)
        ]
        dist = jnp.sqrt(off[0] * off[0] + off[1] * off[1] + off[2] * off[2] + 1.0)
        feat = jnp.where(kind == 0, off[0], jnp.where(kind == 1, off[1], jnp.where(kind == 2, off[2], dist)))
        feat_ref[w * ROWS : (w + 1) * ROWS, :] = feat
    h0 = exact(feat_ref[...], we_ref[0], NN)
    x, r1 = normalise(h0)
    x_ref[...] = x
    r1_ref[...] = r1
    q_ref[...] = exact(x, wq_ref[0, 0], NN) * 0.125
    k_ref[...] = exact(x, wk_ref[0, 0], NN)
    v_ref[...] = three(halves(x), halves(wv_ref[0, 0]), NN)
    key_row = lax.broadcasted_iota(jnp.int32, (ROWS, HEADS * ROWS), 0)

    def attend(w, carry):
        rows = pl.ds(pl.multiple_of(w * ROWS, ROWS), ROWS)
        scores = exact(k_ref[rows, :], spread(q_ref[rows, :], masks), NT)
        scores = jnp.where(key_row < NE, scores, -1e30)
        weights = jnp.exp(scores - jnp.max(scores, axis=0, keepdims=True))
        attention = weights / jnp.sum(weights, axis=0, keepdims=True)
        at_ref[rows, :] = attention
        mixed = three(halves(attention), halves(v_ref[rows, :]), TN)
        mix_ref[rows, :] = gather_heads(mixed, masks)
        return carry

    lax.fori_loop(0, count, attend, 0)
    h1 = h0 + three(halves(mix_ref[...]), halves(wo_ref[0, 0]), NN)
    y, r2 = normalise(h1)
    y_ref[...] = y
    r2_ref[...] = r2
    t = jnp.tanh(three(halves(y), halves(wm_ref[0, 0]), NN) + b_ref[0])
    t_ref[...] = t
    h2 = h1 + t
    real = lax.broadcasted_iota(jnp.int32, (ROWS, 1), 0) < NE
    for w in range(count):
        total = jnp.sum(jnp.where(real, h2[w * ROWS : (w + 1) * ROWS, :], 0.0), axis=0, keepdims=True) / NE
        h2_ref[w : w + 1, :] = total
        la_ref[w : w + 1, :] = jnp.broadcast_to(
            jnp.sum(total * wout_ref[0], axis=1, keepdims=True), (1, 128)
        )


def backward_kernel(
    net_ref, r1_ref, x_ref, q_ref, k_ref, v_ref, at_ref, y_ref, r2_ref, t_ref,
    wq_ref, wk_ref, wv_ref, wo_ref, wm_ref, wout_ref,
    dm_ref, dh1_ref, dqkv_ref, dh0_ref,
    do_ref,
):
    total = x_ref.shape[0]
    count = total // ROWS
    masks = head_masks()
    row = lax.broadcasted_iota(jnp.int32, (total, 1), 0)
    real = (row % ROWS) < NE
    g = jnp.where(real, wout_ref[0] / NE, 0.0)
    t = t_ref[...]
    dm = g * (1.0 - t * t)
    dm_ref[...] = dm
    dy = three(halves(dm), halves(wm_ref[0, 0]), NT)
    dh1 = g + normalise_back(dy, y_ref[...], r2_ref[...])
    dh1_ref[...] = dh1
    do_ref[...] = three(halves(dh1), halves(wo_ref[0, 0]), NT)

    def attend(w, carry):
        rows = pl.ds(pl.multiple_of(w * ROWS, ROWS), ROWS)
        attention = at_ref[rows, :]
        do = halves(spread(do_ref[rows, :], masks))
        da = three(halves(v_ref[rows, :]), do, NT)
        dqkv_ref[rows, 2 * D :] = three(halves(attention), do, NN)
        ds = attention * (da - jnp.sum(da * attention, axis=0, keepdims=True))
        ds = halves(ds)
        dqkv_ref[rows, D : 2 * D] = three(ds, halves(spread(q_ref[rows, :], masks)), NN)
        dqkv_ref[rows, :D] = gather_heads(three(ds, halves(k_ref[rows, :]), TN), masks) * 0.125
        return carry

    lax.fori_loop(0, count, attend, 0)
    dx = three(halves(dqkv_ref[:, :D]), halves(wq_ref[0, 0]), NT)
    dx = dx + three(halves(dqkv_ref[:, D : 2 * D]), halves(wk_ref[0, 0]), NT)
    dx = dx + three(halves(dqkv_ref[:, 2 * D :]), halves(wv_ref[0, 0]), NT)
    dh0_ref[...] = dh1 + normalise_back(dx, x_ref[...], r1_ref[...])


def weights_kernel(x_index_ref, c_ref, feat_ref, x_ref, mix_ref, y_ref, h2_ref, dm_ref, dh1_ref, dqkv_ref, dh0_ref, own_ref, far_ref, up_ref, down_ref, out_ref):
    count = c_ref.shape[0]
    total = x_ref.shape[0]
    factor = jnp.concatenate(
        [jnp.broadcast_to(c_ref[w : w + 1, :1], (ROWS, 1)) for w in range(count)], axis=0
    )
    dm = factor * dm_ref[...]
    def put(i, value):
        for block in range(SPLIT):
            out_ref[block, i * PART : (i + 1) * PART, :] = value[block * PART : (block + 1) * PART, :]

    put(0, three(halves(y_ref[...]), halves(dm), TN))
    put(1, three(halves(mix_ref[...]), halves(factor * dh1_ref[...]), TN))
    x = halves(x_ref[...])
    for i in range(3):
        put(2 + i, three(x, halves(factor * dqkv_ref[:, i * D : (i + 1) * D]), TN))
    base = 5 * PART
    embed = three(halves(feat_ref[...]), halves(factor * dh0_ref[...]), TN)
    for block in range(SPLIT - 1):
        out_ref[block, base:, :] = embed[block * TAIL : (block + 1) * TAIL, :]
    out_ref[SPLIT - 1, base:, :] = jnp.concatenate(
        [
            jnp.sum(dm, axis=0, keepdims=True),
            jnp.sum(c_ref[:, :1] * h2_ref[...], axis=0, keepdims=True),
            jnp.zeros((TAIL - 2, D), jnp.float32),
        ],
        axis=0,
    )
    me = x_index_ref[0]
    for ref, d in ((own_ref, 0), (far_ref, 2), (up_ref, 1), (down_ref, 3)):
        ref[...] = out_ref[(me + d) % SPLIT]


def assemble_kernel(
    where_ref, a0_ref, a1_ref, a2_ref, a3_ref, c0_ref, c1_ref,
    mlp_ref, attn_ref, query_ref, key_ref, value_ref, embed_ref, bias_ref, out_ref,
):
    me, yh = where_ref[0], where_ref[1]
    mats = (mlp_ref, attn_ref, query_ref, key_ref, value_ref)
    for slot, (d, a_ref) in enumerate(((0, a0_ref), (2, a1_ref), (1, a2_ref), (3, a3_ref))):
        block = (me + SPLIT - d) % SPLIT
        start = pl.multiple_of(block * PART, PART)
        for pair, c_ref in enumerate((c0_ref, c1_ref)):
            net = yh if pair == 0 else 1 - yh
            for i in range(5):
                low, high = i * PART, (i + 1) * PART
                cut = min(max(low, HALF), high)
                if cut > low:
                    mats[i][net, pl.ds(start, cut - low), :] = a_ref[pair, low:cut, :]
                if high > cut:
                    mats[i][net, pl.ds(pl.multiple_of(start + (cut - low), 8), high - cut), :] = c_ref[
                        slot, cut - HALF : high - HALF, :
                    ]
            base = 5 * PART - HALF

            @pl.when(block < SPLIT - 1)
            def _():
                embed_ref[net, pl.ds(pl.multiple_of(block * TAIL, TAIL), TAIL), :] = c_ref[slot, base:, :]

            @pl.when(block == SPLIT - 1)
            def _():
                bias_ref[net] = c_ref[slot, base : base + 1, :]
                out_ref[net] = c_ref[slot, base + 1 : base + 2, :]


SPLIT = 4
PART = 64
TAIL = 16
HALF = 168
BLOCK = 336


def vmem():
    return pl.BlockSpec(memory_space=pltpu.VMEM)


def chosen(a):
    zeros = (0,) * (a.ndim - 1)
    return pl.BlockSpec((1,) + a.shape[1:], lambda i, at: (at[0],) + zeros)


def whole(a):
    zeros = (0,) * len(a.shape)
    return pl.BlockSpec(a.shape, lambda i, at: zeros)


def shape(*s):
    return jax.ShapeDtypeStruct(s, jnp.float32)


def call(kernel, outs, at, picked, plain, scratch=()):
    return pl.pallas_call(
        kernel,
        out_shape=outs,
        grid_spec=pltpu.PrefetchScalarGridSpec(
            num_scalar_prefetch=1,
            grid=(1,),
            in_specs=[whole(a) for a in plain] + [chosen(a) for a in picked],
            out_specs=[whole(a) for a in outs],
            scratch_shapes=list(scratch),
        ),
        compiler_params=pltpu.CompilerParams(vmem_limit_bytes=60 * 1024 * 1024),
    )(at, *plain, *picked)


def local(kernel, outs, at, plain, scratch=()):
    return pl.pallas_call(
        kernel,
        out_shape=outs,
        in_specs=[pl.BlockSpec(memory_space=pltpu.SMEM)] + [vmem() for _ in plain],
        out_specs=[vmem() for _ in outs],
        scratch_shapes=list(scratch),
        compiler_params=pltpu.CompilerParams(vmem_limit_bytes=60 * 1024 * 1024),
    )(at, *plain)


def offsets(n):
    return [n // 2] + [d for k in range(1, n // 2) for d in (k, -k)] if n > 2 else [1]


def shift(v, axis, d, n):
    return lax.ppermute(v, axis, [(i, (i + d) % n) for i in range(n)])


def gather(v, axis, n):
    me = lax.axis_index(axis)
    out = jnp.zeros((n,) + v.shape, v.dtype)
    out = lax.dynamic_update_index_in_dim(out, v, me, 0)
    for d in offsets(n):
        out = lax.dynamic_update_index_in_dim(out, shift(v, axis, d, n), (me - d) % n, 0)
    return out


def scatter_sum(v, axis, n):
    me = lax.axis_index(axis)
    blocks = v.reshape((n, v.shape[0] // n) + v.shape[1:])
    total = lax.dynamic_index_in_dim(blocks, me, 0, False)
    for d in offsets(n):
        total = total + shift(lax.dynamic_index_in_dim(blocks, (me + d) % n, 0, False), axis, d, n)
    return total


def everyone(v, axes, n):
    return lax.all_to_all(jnp.broadcast_to(v[None], (n,) + v.shape), axes, 0, 0, tiled=False)


def shards(walkers, nuclei, w_embed, w_query, w_key, w_value, w_attn_out, w_mlp, b_mlp, w_out):
    nx, ny, nz = lax.axis_size("x"), lax.axis_size("yh"), lax.axis_size("z")
    groups = lax.axis_size("ylo") * lax.axis_size("core")
    walker_count = nx * ny * nz
    xi, yh = lax.axis_index("x"), lax.axis_index("yh")
    state = lax.axis_index("ylo") * lax.axis_size("core") + lax.axis_index("core")
    states = 2 * groups
    net = state * 2 + yh
    near = ("ylo", "core", "yh")
    gathered = everyone(walkers.reshape(2, 126), near, groups * ny)
    walk = gathered.reshape(groups, ny, 2, 126).transpose(0, 2, 1, 3).reshape(states * ny, 126)
    nuc = jnp.repeat(nuclei.T, 4, axis=1)
    at = yh.reshape(1).astype(jnp.int32)
    mats = (w_query, w_key, w_value, w_attn_out, w_mlp)
    wout = w_out[:, None, :]
    count = states * ny
    total = count * ROWS
    la, feat, x, r1, q, k, v, atn, mix, y, r2, t, h2 = call(
        forward_kernel,
        [shape(count, 128), shape(total, FEAT), shape(total, D), shape(total, 1), shape(total, D),
         shape(total, D), shape(total, D), shape(total, HEADS * ROWS), shape(total, D),
         shape(total, D), shape(total, 1), shape(total, D), shape(count, D)],
        at, (w_embed,) + mats + (b_mlp, wout), (walk, nuc),
    )
    dm, dh1, dqkv, dh0 = call(
        backward_kernel,
        [shape(total, D), shape(total, D), shape(total, 3 * D), shape(total, D)],
        at, mats + (wout,), (r1, x, q, k, v, atn, y, r2, t),
        [pltpu.VMEM((total, D), jnp.float32)],
    )

    logs = everyone(la[:, 0], near, groups * ny).reshape(states, states, ny)
    home = jnp.diagonal(logs, axis1=0, axis2=1).T
    ratios = jnp.exp(logs - home[None])
    part = jnp.sum(ratios, axis=2).T
    sums = jnp.sum(everyone(part, ("x", "z"), nx * nz), axis=0)
    margins = sums / walker_count
    identity = jnp.eye(states, dtype=jnp.float32)
    coupling = margins.T * (1.0 - identity)
    denominator = jnp.sum(coupling[:, :, None] * ratios.transpose(1, 0, 2), axis=1) / walker_count
    cot = coupling.T[:, :, None] * ratios / walker_count - identity[:, :, None] * denominator[None]
    own = lax.dynamic_index_in_dim(cot, net, 0, False).reshape(count)
    own = jnp.broadcast_to(own[:, None], (count, 128))

    block = shape(BLOCK, D)
    pieces = local(
        weights_kernel, [block] * 4, xi.reshape(1).astype(jnp.int32),
        (own, feat, x, mix, y, h2, dm, dh1, dqkv, dh0),
        [pltpu.VMEM((SPLIT, BLOCK, D), jnp.float32)],
    )
    mine = pieces[0]
    for d, piece in zip((2, 1, -1), pieces[1:]):
        mine = mine + shift(piece, "x", d, nx)
    mine = gather(scatter_sum(mine, "z", nz), "z", nz).reshape(BLOCK, D)
    a, c = mine[:HALF], mine[HALF:]
    a = jnp.stack([a, shift(a, "yh", 1, ny)])
    c = jnp.stack([c] + [shift(c, "x", d, nx) for d in (2, 1, -1)])
    arrays = [a] + [shift(a, "x", d, nx) for d in (2, 1, -1)] + [c, shift(c, "yh", 1, ny)]
    mat = shape(2, D, D)
    mlp, attn, query, key, value, embed, bias, out = local(
        assemble_kernel, [mat] * 5 + [shape(2, FEAT, D), shape(2, 1, D), shape(2, 1, D)],
        jnp.stack([xi, yh]).astype(jnp.int32), arrays,
    )
    return (
        margins, embed, query[:, None], key[:, None], value[:, None],
        attn[:, None], mlp[:, None], bias, out[:, 0],
    )


def solution(mesh):
    fine = Mesh(mesh.devices.reshape(2, 2, 4, 2, 8), ("ylo", "core", "x", "yh", "z"))
    s, w = ("ylo", "core"), ("x", "yh", "z")
    return jax.shard_map(
        shards,
        mesh=fine,
        in_specs=(P(s, w, None), P()) + (P(s),) * 8,
        out_specs=(P(),) + (P(s),) * 8,
        check_vma=False,
    )
```

```python
import jax
import jax.numpy as jnp
from jax import lax
from jax.experimental import pallas as pl
from jax.experimental.pallas import tpu as pltpu
from jax.sharding import Mesh, PartitionSpec as P

HEADS = 4
NE = 42
ROWS = 48
D = 256
FEAT = 48
EPS = 1e-05
HIGHEST = lax.Precision.HIGHEST
NN = (((1,), (0,)), ((), ()))
NT = (((1,), (1,)), ((), ()))
TN = (((0,), (0,)), ((), ()))
UNROLL = 4


def exact(a, b, dims):
    return lax.dot_general(a, b, dims, precision=HIGHEST, preferred_element_type=jnp.float32)


def halves(a):
    high = a.astype(jnp.bfloat16)
    return high, (a - high.astype(jnp.float32)).astype(jnp.bfloat16)


def three(a, b, dims):
    def one(x, y):
        return lax.dot_general(x, y, dims, preferred_element_type=jnp.float32)

    return one(a[0], b[0]) + (one(a[0], b[1]) + one(a[1], b[0]))


def stacked_tn(a, b):
    left = jnp.concatenate([a[0], a[0], a[1]], axis=0)
    right = jnp.concatenate([b[0], b[1], b[0]], axis=0)
    return lax.dot_general(left, right, TN, preferred_element_type=jnp.float32)


def normalise(hidden):
    centre = hidden - jnp.mean(hidden, axis=-1, keepdims=True)
    scale = lax.rsqrt(jnp.mean(centre * centre, axis=-1, keepdims=True) + EPS)
    return centre * scale, scale


def normalise_back(grad, normed, scale):
    return scale * (
        grad
        - jnp.mean(grad, axis=-1, keepdims=True)
        - normed * jnp.mean(grad * normed, axis=-1, keepdims=True)
    )


def head_masks():
    lane = lax.broadcasted_iota(jnp.int32, (1, D), 1)
    return [(lane // (D // HEADS)) == h for h in range(HEADS)]


def spread(block, masks):
    return jnp.concatenate([jnp.where(m, block, 0.0) for m in masks], axis=0)


def gather_heads(stacked, masks):
    out = jnp.where(masks[0], stacked[:ROWS], 0.0)
    for h in range(1, HEADS):
        out = out + jnp.where(masks[h], stacked[h * ROWS : (h + 1) * ROWS], 0.0)
    return out


def fetch(source, target, sem):
    copy = pltpu.make_async_copy(source, target, sem)
    copy.start()
    return copy


def forward_kernel(
    net_ref, walk_ref, nuc_ref, b_ref, wout_ref, we_hbm, wq_hbm, wk_hbm, wv_hbm, wo_hbm, wm_hbm,
    la_ref, h2_ref, feat_hbm, x_hbm, q_hbm, k_hbm, v_hbm, at_hbm, mix_hbm, y_hbm, t_hbm,
    we_ref, w_ref, feat_ref, x_ref, q_ref, k_ref, v_ref, at_ref, mix_ref, y_ref, t_ref, in_sem, out_sem,
):
    at = net_ref[0]
    loads = [fetch(we_hbm.at[at], we_ref, in_sem.at[0])]
    for i, w in enumerate((wq_hbm, wk_hbm, wv_hbm, wo_hbm, wm_hbm)):
        loads.append(fetch(w.at[at, 0], w_ref.at[i], in_sem.at[1 + i]))
    count = walk_ref.shape[0]
    width = walk_ref.shape[1]
    electron = lax.broadcasted_iota(jnp.int32, (ROWS, width), 0)
    lane = lax.broadcasted_iota(jnp.int32, (ROWS, width), 1)
    picks = [lane == 3 * electron + c for c in range(3)]
    flane = lax.broadcasted_iota(jnp.int32, (1, FEAT), 1)
    kind = flane % 4
    masks = head_masks()
    n = [nuc_ref[c : c + 1, :] for c in range(3)]
    for w in range(count):
        row = jnp.broadcast_to(walk_ref[w : w + 1, :], (ROWS, width))
        off = [
            jnp.sum(jnp.where(picks[c], row, 0.0), axis=1, keepdims=True) - n[c] for c in range(3)
        ]
        dist = jnp.sqrt(off[0] * off[0] + off[1] * off[1] + off[2] * off[2] + 1.0)
        feat = jnp.where(kind == 0, off[0], jnp.where(kind == 1, off[1], jnp.where(kind == 2, off[2], dist)))
        feat_ref[w * ROWS : (w + 1) * ROWS, :FEAT] = feat
    loads[0].wait()
    h0 = exact(feat_ref[:, :FEAT], we_ref[...], NN)
    x, r1 = normalise(h0)
    feat_ref[:, FEAT : FEAT + 1] = r1
    x_ref[...] = x
    stores = [fetch(x_ref, x_hbm, out_sem.at[0])]
    loads[1].wait()
    q_ref[...] = exact(x, w_ref[0], NN) * 0.125
    stores.append(fetch(q_ref, q_hbm, out_sem.at[1]))
    loads[2].wait()
    k_ref[...] = exact(x, w_ref[1], NN)
    stores.append(fetch(k_ref, k_hbm, out_sem.at[2]))
    loads[3].wait()
    v_ref[...] = three(halves(x), halves(w_ref[2]), NN)
    stores.append(fetch(v_ref, v_hbm, out_sem.at[3]))
    key_row = lax.broadcasted_iota(jnp.int32, (ROWS, HEADS * ROWS), 0)

    def attend(step, carry):
        spans = [
            pl.ds(pl.multiple_of(step * (UNROLL * ROWS) + u * ROWS, ROWS), ROWS) for u in range(UNROLL)
        ]
        scores = [exact(k_ref[rows, :], spread(q_ref[rows, :], masks), NT) for rows in spans]
        scores = [jnp.where(key_row < NE, a, -1e30) for a in scores]
        weights = [jnp.exp(a - jnp.max(a, axis=0, keepdims=True)) for a in scores]
        attention = [a / jnp.sum(a, axis=0, keepdims=True) for a in weights]
        for rows, a in zip(spans, attention):
            at_ref[rows, :] = a
        mixed = [stacked_tn(halves(a), halves(v_ref[rows, :])) for rows, a in zip(spans, attention)]
        for rows, a in zip(spans, mixed):
            mix_ref[rows, :] = gather_heads(a, masks)
        return carry

    lax.fori_loop(0, count // UNROLL, attend, 0)
    stores.append(fetch(at_ref, at_hbm, out_sem.at[4]))
    stores.append(fetch(mix_ref, mix_hbm, out_sem.at[5]))
    loads[4].wait()
    h1 = h0 + three(halves(mix_ref[...]), halves(w_ref[3]), NN)
    y, r2 = normalise(h1)
    feat_ref[:, FEAT + 1 : FEAT + 2] = r2
    stores.append(fetch(feat_ref, feat_hbm, out_sem.at[6]))
    y_ref[...] = y
    stores.append(fetch(y_ref, y_hbm, out_sem.at[7]))
    loads[5].wait()
    t = jnp.tanh(three(halves(y), halves(w_ref[4]), NN) + b_ref[at])
    t_ref[...] = t
    stores.append(fetch(t_ref, t_hbm, out_sem.at[8]))
    h2 = h1 + t
    real = lax.broadcasted_iota(jnp.int32, (ROWS, 1), 0) < NE
    for w in range(count):
        total = jnp.sum(jnp.where(real, h2[w * ROWS : (w + 1) * ROWS, :], 0.0), axis=0, keepdims=True) / NE
        h2_ref[w : w + 1, :] = total
        la_ref[w : w + 1, :] = jnp.broadcast_to(
            jnp.sum(total * wout_ref[at], axis=1, keepdims=True), (1, 128)
        )
    for copy in stores:
        copy.wait()


def backward_kernel(
    where_ref, c_ref, h2_ref, wout_ref,
    feat_hbm, x_hbm, q_hbm, k_hbm, v_hbm, at_hbm, mix_hbm, y_hbm, t_hbm,
    wq_hbm, wk_hbm, wv_hbm, wo_hbm, wm_hbm,
    own_ref, far_ref, up_ref, down_ref,
    w_ref, feat_ref, x_ref, q_ref, k_ref, v_ref, at_ref, mix_ref, y_ref, t_ref,
    do_ref, dqkv_ref, out_ref, sem,
):
    me, at = where_ref[0], where_ref[1]
    order = (
        (t_hbm, t_ref), (wm_hbm.at[at, 0], w_ref.at[4]), (y_hbm, y_ref), (feat_hbm, feat_ref),
        (wo_hbm.at[at, 0], w_ref.at[3]), (at_hbm, at_ref), (v_hbm, v_ref), (q_hbm, q_ref), (k_hbm, k_ref),
        (wq_hbm.at[at, 0], w_ref.at[0]), (wk_hbm.at[at, 0], w_ref.at[1]), (wv_hbm.at[at, 0], w_ref.at[2]),
        (x_hbm, x_ref), (mix_hbm, mix_ref),
    )
    loads = [fetch(a, b, sem.at[i]) for i, (a, b) in enumerate(order)]
    count = c_ref.shape[0]
    masks = head_masks()
    real = lax.broadcasted_iota(jnp.int32, (ROWS, 1), 0) < NE
    factor = jnp.concatenate(
        [jnp.where(real, c_ref[w : w + 1, :1] / NE, 0.0) for w in range(count)], axis=0
    )

    def put(i, value):
        for block in range(SPLIT):
            out_ref[block, i * PART : (i + 1) * PART, :] = value[block * PART : (block + 1) * PART, :]

    g = factor * wout_ref[at]
    loads[0].wait()
    t = t_ref[...]
    dm = g * (1.0 - t * t)
    dm_parts = halves(dm)
    loads[1].wait()
    dy = three(dm_parts, halves(w_ref[4]), NT)
    loads[2].wait()
    loads[3].wait()
    y = y_ref[...]
    put(0, three(halves(y), dm_parts, TN))
    dh1 = g + normalise_back(dy, y, feat_ref[:, FEAT + 1 : FEAT + 2])
    dh1_parts = halves(dh1)
    loads[4].wait()
    do_ref[...] = three(dh1_parts, halves(w_ref[3]), NT)
    for copy in loads[5:9]:
        copy.wait()

    def attend(step, carry):
        spans = [
            pl.ds(pl.multiple_of(step * (UNROLL * ROWS) + u * ROWS, ROWS), ROWS) for u in range(UNROLL)
        ]
        attention = [at_ref[rows, :] for rows in spans]
        do = [halves(spread(do_ref[rows, :], masks)) for rows in spans]
        da = [three(halves(v_ref[rows, :]), a, NT) for rows, a in zip(spans, do)]
        dv = [three(halves(a), b, NN) for a, b in zip(attention, do)]
        ds = [a * (b - jnp.sum(b * a, axis=0, keepdims=True)) for a, b in zip(attention, da)]
        ds = [halves(a) for a in ds]
        dk = [three(a, halves(spread(q_ref[rows, :], masks)), NN) for rows, a in zip(spans, ds)]
        dq = [stacked_tn(a, halves(k_ref[rows, :])) for rows, a in zip(spans, ds)]
        for rows, a, b, c in zip(spans, dq, dk, dv):
            dqkv_ref[rows, :D] = gather_heads(a, masks) * 0.125
            dqkv_ref[rows, D : 2 * D] = b
            dqkv_ref[rows, 2 * D :] = c
        return carry

    lax.fori_loop(0, count // UNROLL, attend, 0)
    for copy in loads[9:13]:
        copy.wait()
    x = x_ref[...]
    x_parts = halves(x)
    dx = None
    for i in range(3):
        part = halves(dqkv_ref[:, i * D : (i + 1) * D])
        term = three(part, halves(w_ref[i]), NT)
        dx = term if dx is None else dx + term
        put(2 + i, three(x_parts, part, TN))
    loads[13].wait()
    put(1, three(halves(mix_ref[...]), dh1_parts, TN))
    dh0 = dh1 + normalise_back(dx, x, feat_ref[:, FEAT : FEAT + 1])
    base = 5 * PART
    embed = three(halves(feat_ref[:, :FEAT]), halves(dh0), TN)
    for block in range(SPLIT - 1):
        out_ref[block, base:, :] = embed[block * TAIL : (block + 1) * TAIL, :]
    out_ref[SPLIT - 1, base:, :] = jnp.concatenate(
        [
            jnp.sum(dm, axis=0, keepdims=True),
            jnp.sum(c_ref[:, :1] * h2_ref[...], axis=0, keepdims=True),
            jnp.zeros((TAIL - 2, D), jnp.float32),
        ],
        axis=0,
    )
    for ref, d in ((own_ref, 0), (far_ref, 2), (up_ref, 1), (down_ref, 3)):
        ref[...] = out_ref[(me + d) % SPLIT]


def assemble_kernel(
    where_ref, a0_ref, a1_ref, a2_ref, a3_ref, c0_ref, c1_ref,
    mlp_ref, attn_ref, query_ref, key_ref, value_ref, embed_ref, bias_ref, out_ref,
):
    me, yh = where_ref[0], where_ref[1]
    mats = (mlp_ref, attn_ref, query_ref, key_ref, value_ref)
    for slot, (d, a_ref) in enumerate(((0, a0_ref), (2, a1_ref), (1, a2_ref), (3, a3_ref))):
        block = (me + SPLIT - d) % SPLIT
        start = pl.multiple_of(block * PART, PART)
        for pair, c_ref in enumerate((c0_ref, c1_ref)):
            net = yh if pair == 0 else 1 - yh
            for i in range(5):
                low, high = i * PART, (i + 1) * PART
                cut = min(max(low, HALF), high)
                if cut > low:
                    mats[i][net, pl.ds(start, cut - low), :] = a_ref[pair, low:cut, :]
                if high > cut:
                    mats[i][net, pl.ds(pl.multiple_of(start + (cut - low), 8), high - cut), :] = c_ref[
                        slot, cut - HALF : high - HALF, :
                    ]
            base = 5 * PART - HALF

            @pl.when(block < SPLIT - 1)
            def _():
                embed_ref[net, pl.ds(pl.multiple_of(block * TAIL, TAIL), TAIL), :] = c_ref[slot, base:, :]

            @pl.when(block == SPLIT - 1)
            def _():
                bias_ref[net] = c_ref[slot, base : base + 1, :]
                out_ref[net] = c_ref[slot, base + 1 : base + 2, :]


SPLIT = 4
PART = 64
TAIL = 16
HALF = 168
BLOCK = 336


def vmem():
    return pl.BlockSpec(memory_space=pltpu.VMEM)


def shape(*s):
    return jax.ShapeDtypeStruct(s, jnp.float32)


def local(kernel, outs, at, plain, limit, far=(), far_outs=(), scratch=()):
    anywhere = pl.BlockSpec(memory_space=pltpu.MemorySpace.HBM)
    return pl.pallas_call(
        kernel,
        out_shape=list(outs) + list(far_outs),
        in_specs=[pl.BlockSpec(memory_space=pltpu.SMEM)] + [vmem() for _ in plain] + [anywhere for _ in far],
        out_specs=[vmem() for _ in outs] + [anywhere for _ in far_outs],
        scratch_shapes=list(scratch),
        compiler_params=pltpu.CompilerParams(vmem_limit_bytes=limit * 1024 * 1024),
    )(at, *plain, *far)


def offsets(n):
    return [n // 2] + [d for k in range(1, n // 2) for d in (k, -k)] if n > 2 else [1]


def shift(v, axis, d, n):
    return lax.ppermute(v, axis, [(i, (i + d) % n) for i in range(n)])


def gather(v, axis, n):
    me = lax.axis_index(axis)
    out = jnp.zeros((n,) + v.shape, v.dtype)
    out = lax.dynamic_update_index_in_dim(out, v, me, 0)
    for d in offsets(n):
        out = lax.dynamic_update_index_in_dim(out, shift(v, axis, d, n), (me - d) % n, 0)
    return out


def scatter_sum(v, axis, n):
    me = lax.axis_index(axis)
    blocks = v.reshape((n, v.shape[0] // n) + v.shape[1:])
    total = lax.dynamic_index_in_dim(blocks, me, 0, False)
    for d in offsets(n):
        total = total + shift(lax.dynamic_index_in_dim(blocks, (me + d) % n, 0, False), axis, d, n)
    return total


def everyone(v, axes, n):
    return lax.all_to_all(jnp.broadcast_to(v[None], (n,) + v.shape), axes, 0, 0, tiled=False)


def shards(walkers, nuclei, w_embed, w_query, w_key, w_value, w_attn_out, w_mlp, b_mlp, w_out):
    nx, ny, nz = lax.axis_size("x"), lax.axis_size("yh"), lax.axis_size("z")
    groups = lax.axis_size("ylo") * lax.axis_size("core")
    walker_count = nx * ny * nz
    xi, yh = lax.axis_index("x"), lax.axis_index("yh")
    state = lax.axis_index("ylo") * lax.axis_size("core") + lax.axis_index("core")
    states = 2 * groups
    net = state * 2 + yh
    near = ("ylo", "core", "yh")
    gathered = everyone(walkers.reshape(2, 126), near, groups * ny)
    walk = gathered.reshape(groups, ny, 2, 126).transpose(0, 2, 1, 3).reshape(states * ny, 126)
    nuc = jnp.repeat(nuclei.T, 4, axis=1)
    at = yh.reshape(1).astype(jnp.int32)
    mats = (w_query, w_key, w_value, w_attn_out, w_mlp)
    wout = w_out[:, None, :]
    count = states * ny
    total = count * ROWS
    saved = [shape(total, 128)] + [shape(total, D)] * 4 + [shape(total, HEADS * ROWS)] + [shape(total, D)] * 3
    rooms = [pltpu.VMEM(a.shape, jnp.float32) for a in saved]
    la, h2, *kept = local(
        forward_kernel, [shape(count, 128), shape(count, D)], at, (walk, nuc, b_mlp, wout), 40,
        (w_embed,) + mats, saved,
        [pltpu.VMEM((FEAT, D), jnp.float32), pltpu.VMEM((5, D, D), jnp.float32)]
        + rooms
        + [pltpu.SemaphoreType.DMA((6,)), pltpu.SemaphoreType.DMA((9,))],
    )

    logs = everyone(la[:, 0], near, groups * ny).reshape(states, states, ny)
    home = jnp.diagonal(logs, axis1=0, axis2=1).T
    ratios = jnp.exp(logs - home[None])
    part = jnp.sum(ratios, axis=2).T
    sums = jnp.sum(everyone(part, ("x", "z"), nx * nz), axis=0)
    margins = sums / walker_count
    identity = jnp.eye(states, dtype=jnp.float32)
    coupling = margins.T * (1.0 - identity)
    denominator = jnp.sum(coupling[:, :, None] * ratios.transpose(1, 0, 2), axis=1) / walker_count
    cot = coupling.T[:, :, None] * ratios / walker_count - identity[:, :, None] * denominator[None]
    own = lax.dynamic_index_in_dim(cot, net, 0, False).reshape(count)
    own = jnp.broadcast_to(own[:, None], (count, 128))

    place = jnp.stack([xi, yh]).astype(jnp.int32)
    pieces = local(
        backward_kernel, [shape(BLOCK, D)] * 4, place, (own, h2, wout), 50,
        tuple(kept) + mats, (),
        [pltpu.VMEM((5, D, D), jnp.float32)]
        + rooms
        + [pltpu.VMEM((total, D), jnp.float32), pltpu.VMEM((total, 3 * D), jnp.float32),
           pltpu.VMEM((SPLIT, BLOCK, D), jnp.float32), pltpu.SemaphoreType.DMA((14,))],
    )
    mine = pieces[0]
    for d, piece in zip((2, 1, -1), pieces[1:]):
        mine = mine + shift(piece, "x", d, nx)
    mine = gather(scatter_sum(mine, "z", nz), "z", nz).reshape(BLOCK, D)
    a, c = mine[:HALF], mine[HALF:]
    a_far = shift(a, "yh", 1, ny)
    c_far = [shift(c, "x", d, nx) for d in (2, 1, -1)]
    a_far, *c_far = lax.optimization_barrier((a_far, *c_far))
    a = jnp.stack([a, a_far])
    c = jnp.stack([c, *c_far])
    arrays = [a] + [shift(a, "x", d, nx) for d in (2, 1, -1)] + [c, shift(c, "yh", 1, ny)]
    mat = shape(2, D, D)
    mlp, attn, query, key, value, embed, bias, out = local(
        assemble_kernel, [mat] * 5 + [shape(2, FEAT, D), shape(2, 1, D), shape(2, 1, D)],
        place, arrays, 4,
    )
    return (
        margins, embed, query[:, None], key[:, None], value[:, None],
        attn[:, None], mlp[:, None], bias, out[:, 0],
    )


def solution(mesh):
    fine = Mesh(mesh.devices.reshape(2, 2, 4, 2, 8), ("ylo", "core", "x", "yh", "z"))
    s, w = ("ylo", "core"), ("x", "yh", "z")
    return jax.shard_map(
        shards,
        mesh=fine,
        in_specs=(P(s, w, None), P()) + (P(s),) * 8,
        out_specs=(P(),) + (P(s),) * 8,
        check_vma=False,
    )
```

```python
import jax
import jax.numpy as jnp
from jax import lax
from jax.experimental import pallas as pl
from jax.experimental.pallas import tpu as pltpu
from jax.sharding import Mesh, PartitionSpec as P

HEADS = 4
NE = 42
ROWS = 48
D = 256
FEAT = 48
EPS = 1e-05
HIGHEST = lax.Precision.HIGHEST
NN = (((1,), (0,)), ((), ()))
NT = (((1,), (1,)), ((), ()))
TN = (((0,), (0,)), ((), ()))
UNROLL = 4


def exact(a, b, dims):
    return lax.dot_general(a, b, dims, precision=HIGHEST, preferred_element_type=jnp.float32)


def halves(a):
    high = a.astype(jnp.bfloat16)
    return high, (a - high.astype(jnp.float32)).astype(jnp.bfloat16)


def three(a, b, dims):
    def one(x, y):
        return lax.dot_general(x, y, dims, preferred_element_type=jnp.float32)

    return one(a[0], b[0]) + (one(a[0], b[1]) + one(a[1], b[0]))


def stacked_tn(a, b):
    left = jnp.concatenate([a[0], a[0], a[1]], axis=0)
    right = jnp.concatenate([b[0], b[1], b[0]], axis=0)
    return lax.dot_general(left, right, TN, preferred_element_type=jnp.float32)


def normalise(hidden):
    centre = hidden - jnp.mean(hidden, axis=-1, keepdims=True)
    scale = lax.rsqrt(jnp.mean(centre * centre, axis=-1, keepdims=True) + EPS)
    return centre * scale, scale


def normalise_back(grad, normed, scale):
    return scale * (
        grad
        - jnp.mean(grad, axis=-1, keepdims=True)
        - normed * jnp.mean(grad * normed, axis=-1, keepdims=True)
    )


def head_masks():
    lane = lax.broadcasted_iota(jnp.int32, (1, D), 1)
    return [(lane // (D // HEADS)) == h for h in range(HEADS)]


def spread(block, masks):
    return jnp.concatenate([jnp.where(m, block, 0.0) for m in masks], axis=0)


def gather_heads(stacked, masks):
    out = jnp.where(masks[0], stacked[:ROWS], 0.0)
    for h in range(1, HEADS):
        out = out + jnp.where(masks[h], stacked[h * ROWS : (h + 1) * ROWS], 0.0)
    return out


def fetch(source, target, sem):
    copy = pltpu.make_async_copy(source, target, sem)
    copy.start()
    return copy


def forward_kernel(
    net_ref, walk_ref, nuc_ref, b_ref, wout_ref, we_hbm, wq_hbm, wk_hbm, wv_hbm, wo_hbm, wm_hbm,
    la_ref, h2_ref, feat_hbm, x_hbm, q_hbm, k_hbm, v_hbm, at_hbm, mix_hbm, y_hbm, t_hbm,
    we_ref, w_ref, feat_ref, x_ref, q_ref, k_ref, v_ref, at_ref, mix_ref, y_ref, t_ref, in_sem, out_sem,
):
    at = net_ref[0]
    loads = [fetch(we_hbm.at[at], we_ref, in_sem.at[0])]
    for i, w in enumerate((wq_hbm, wk_hbm, wv_hbm, wo_hbm, wm_hbm)):
        loads.append(fetch(w.at[at, 0], w_ref.at[i], in_sem.at[1 + i]))
    count = walk_ref.shape[0]
    width = walk_ref.shape[1]
    electron = lax.broadcasted_iota(jnp.int32, (ROWS, width), 0)
    lane = lax.broadcasted_iota(jnp.int32, (ROWS, width), 1)
    picks = [lane == 3 * electron + c for c in range(3)]
    flane = lax.broadcasted_iota(jnp.int32, (1, FEAT), 1)
    kind = flane % 4
    masks = head_masks()
    n = [nuc_ref[c : c + 1, :] for c in range(3)]
    for w in range(count):
        row = jnp.broadcast_to(walk_ref[w : w + 1, :], (ROWS, width))
        off = [
            jnp.sum(jnp.where(picks[c], row, 0.0), axis=1, keepdims=True) - n[c] for c in range(3)
        ]
        dist = jnp.sqrt(off[0] * off[0] + off[1] * off[1] + off[2] * off[2] + 1.0)
        feat = jnp.where(kind == 0, off[0], jnp.where(kind == 1, off[1], jnp.where(kind == 2, off[2], dist)))
        feat_ref[w * ROWS : (w + 1) * ROWS, :FEAT] = feat
    loads[0].wait()
    h0 = exact(feat_ref[:, :FEAT], we_ref[...], NN)
    x, r1 = normalise(h0)
    feat_ref[:, FEAT : FEAT + 1] = r1
    x_ref[...] = x
    stores = [fetch(x_ref, x_hbm, out_sem.at[0])]
    loads[1].wait()
    q_ref[...] = exact(x, w_ref[0], NN) * 0.125
    stores.append(fetch(q_ref, q_hbm, out_sem.at[1]))
    loads[2].wait()
    k_ref[...] = exact(x, w_ref[1], NN)
    stores.append(fetch(k_ref, k_hbm, out_sem.at[2]))
    loads[3].wait()
    v_ref[...] = three(halves(x), halves(w_ref[2]), NN)
    stores.append(fetch(v_ref, v_hbm, out_sem.at[3]))
    key_row = lax.broadcasted_iota(jnp.int32, (ROWS, HEADS * ROWS), 0)

    def attend(step, carry):
        spans = [
            pl.ds(pl.multiple_of(step * (UNROLL * ROWS) + u * ROWS, ROWS), ROWS) for u in range(UNROLL)
        ]
        scores = [exact(k_ref[rows, :], spread(q_ref[rows, :], masks), NT) for rows in spans]
        scores = [jnp.where(key_row < NE, a, -1e30) for a in scores]
        weights = [jnp.exp(a - jnp.max(a, axis=0, keepdims=True)) for a in scores]
        attention = [a / jnp.sum(a, axis=0, keepdims=True) for a in weights]
        for rows, a in zip(spans, attention):
            at_ref[rows, :] = a
        mixed = [stacked_tn(halves(a), halves(v_ref[rows, :])) for rows, a in zip(spans, attention)]
        for rows, a in zip(spans, mixed):
            mix_ref[rows, :] = gather_heads(a, masks)
        return carry

    lax.fori_loop(0, count // UNROLL, attend, 0)
    stores.append(fetch(at_ref, at_hbm, out_sem.at[4]))
    stores.append(fetch(mix_ref, mix_hbm, out_sem.at[5]))
    loads[4].wait()
    h1 = h0 + three(halves(mix_ref[...]), halves(w_ref[3]), NN)
    y, r2 = normalise(h1)
    feat_ref[:, FEAT + 1 : FEAT + 2] = r2
    stores.append(fetch(feat_ref, feat_hbm, out_sem.at[6]))
    y_ref[...] = y
    stores.append(fetch(y_ref, y_hbm, out_sem.at[7]))
    loads[5].wait()
    t = jnp.tanh(three(halves(y), halves(w_ref[4]), NN) + b_ref[at])
    t_ref[...] = t
    stores.append(fetch(t_ref, t_hbm, out_sem.at[8]))
    h2 = h1 + t
    real = lax.broadcasted_iota(jnp.int32, (ROWS, 1), 0) < NE
    for w in range(count):
        total = jnp.sum(jnp.where(real, h2[w * ROWS : (w + 1) * ROWS, :], 0.0), axis=0, keepdims=True) / NE
        h2_ref[w : w + 1, :] = total
        la_ref[w : w + 1, :] = jnp.broadcast_to(
            jnp.sum(total * wout_ref[at], axis=1, keepdims=True), (1, 128)
        )
    for copy in stores:
        copy.wait()


def backward_kernel(
    where_ref, c_ref, h2_ref, wout_ref,
    feat_hbm, x_hbm, q_hbm, k_hbm, v_hbm, at_hbm, mix_hbm, y_hbm, t_hbm,
    wq_hbm, wk_hbm, wv_hbm, wo_hbm, wm_hbm,
    own_ref, far_ref, up_ref, down_ref,
    w_ref, feat_ref, x_ref, q_ref, k_ref, v_ref, at_ref, mix_ref, y_ref, t_ref,
    do_ref, dqkv_ref, out_ref, sem,
):
    me, at = where_ref[0], where_ref[1]
    order = (
        (t_hbm, t_ref), (wm_hbm.at[at, 0], w_ref.at[4]), (y_hbm, y_ref), (feat_hbm, feat_ref),
        (wo_hbm.at[at, 0], w_ref.at[3]), (at_hbm, at_ref), (v_hbm, v_ref), (q_hbm, q_ref), (k_hbm, k_ref),
        (wq_hbm.at[at, 0], w_ref.at[0]), (wk_hbm.at[at, 0], w_ref.at[1]), (wv_hbm.at[at, 0], w_ref.at[2]),
        (x_hbm, x_ref), (mix_hbm, mix_ref),
    )
    loads = [fetch(a, b, sem.at[i]) for i, (a, b) in enumerate(order)]
    count = c_ref.shape[0]
    masks = head_masks()
    real = lax.broadcasted_iota(jnp.int32, (ROWS, 1), 0) < NE
    factor = jnp.concatenate(
        [jnp.where(real, c_ref[w : w + 1, :1] / NE, 0.0) for w in range(count)], axis=0
    )

    def put(i, value):
        for block in range(SPLIT):
            out_ref[block, i * PART : (i + 1) * PART, :] = value[block * PART : (block + 1) * PART, :]

    g = factor * wout_ref[at]
    loads[0].wait()
    t = t_ref[...]
    dm = g * (1.0 - t * t)
    dm_parts = halves(dm)
    loads[1].wait()
    dy = three(dm_parts, halves(w_ref[4]), NT)
    loads[2].wait()
    loads[3].wait()
    y = y_ref[...]
    put(0, three(halves(y), dm_parts, TN))
    dh1 = g + normalise_back(dy, y, feat_ref[:, FEAT + 1 : FEAT + 2])
    dh1_parts = halves(dh1)
    loads[4].wait()
    do_ref[...] = three(dh1_parts, halves(w_ref[3]), NT)
    for copy in loads[5:9]:
        copy.wait()

    def attend(step, carry):
        spans = [
            pl.ds(pl.multiple_of(step * (UNROLL * ROWS) + u * ROWS, ROWS), ROWS) for u in range(UNROLL)
        ]
        attention = [at_ref[rows, :] for rows in spans]
        do = [halves(spread(do_ref[rows, :], masks)) for rows in spans]
        da = [three(halves(v_ref[rows, :]), a, NT) for rows, a in zip(spans, do)]
        dv = [three(halves(a), b, NN) for a, b in zip(attention, do)]
        ds = [a * (b - jnp.sum(b * a, axis=0, keepdims=True)) for a, b in zip(attention, da)]
        ds = [halves(a) for a in ds]
        dk = [three(a, halves(spread(q_ref[rows, :], masks)), NN) for rows, a in zip(spans, ds)]
        dq = [stacked_tn(a, halves(k_ref[rows, :])) for rows, a in zip(spans, ds)]
        for rows, a, b, c in zip(spans, dq, dk, dv):
            dqkv_ref[rows, :D] = gather_heads(a, masks) * 0.125
            dqkv_ref[rows, D : 2 * D] = b
            dqkv_ref[rows, 2 * D :] = c
        return carry

    lax.fori_loop(0, count // UNROLL, attend, 0)
    for copy in loads[9:13]:
        copy.wait()
    x = x_ref[...]
    x_parts = halves(x)
    dx = None
    for i in range(3):
        part = halves(dqkv_ref[:, i * D : (i + 1) * D])
        term = three(part, halves(w_ref[i]), NT)
        dx = term if dx is None else dx + term
        put(2 + i, three(x_parts, part, TN))
    loads[13].wait()
    put(1, three(halves(mix_ref[...]), dh1_parts, TN))
    dh0 = dh1 + normalise_back(dx, x, feat_ref[:, FEAT : FEAT + 1])
    base = 5 * PART
    embed = three(halves(feat_ref[:, :FEAT]), halves(dh0), TN)
    for block in range(SPLIT - 1):
        out_ref[block, base:, :] = embed[block * TAIL : (block + 1) * TAIL, :]
    out_ref[SPLIT - 1, base:, :] = jnp.concatenate(
        [
            jnp.sum(dm, axis=0, keepdims=True),
            jnp.sum(c_ref[:, :1] * h2_ref[...], axis=0, keepdims=True),
            jnp.zeros((TAIL - 2, D), jnp.float32),
        ],
        axis=0,
    )
    for ref, d in ((own_ref, 0), (far_ref, 2), (up_ref, 1), (down_ref, 3)):
        ref[...] = out_ref[(me + d) % SPLIT]


def assemble_kernel(
    where_ref, a0_ref, a1_ref, a2_ref, a3_ref, c0_ref, c1_ref,
    mlp_ref, attn_ref, query_ref, key_ref, value_ref, embed_ref, bias_ref, out_ref,
):
    me, yh = where_ref[0], where_ref[1]
    mats = (mlp_ref, attn_ref, query_ref, key_ref, value_ref)
    for slot, (d, a_ref) in enumerate(((0, a0_ref), (2, a1_ref), (1, a2_ref), (3, a3_ref))):
        block = (me + SPLIT - d) % SPLIT
        start = pl.multiple_of(block * PART, PART)
        for pair, c_ref in enumerate((c0_ref, c1_ref)):
            net = yh if pair == 0 else 1 - yh
            for i in range(5):
                low, high = i * PART, (i + 1) * PART
                cut = min(max(low, HALF), high)
                if cut > low:
                    mats[i][net, pl.ds(start, cut - low), :] = a_ref[pair, low:cut, :]
                if high > cut:
                    mats[i][net, pl.ds(pl.multiple_of(start + (cut - low), 8), high - cut), :] = c_ref[
                        slot, cut - HALF : high - HALF, :
                    ]
            base = 5 * PART - HALF

            @pl.when(block < SPLIT - 1)
            def _():
                embed_ref[net, pl.ds(pl.multiple_of(block * TAIL, TAIL), TAIL), :] = c_ref[slot, base:, :]

            @pl.when(block == SPLIT - 1)
            def _():
                bias_ref[net] = c_ref[slot, base : base + 1, :]
                out_ref[net] = c_ref[slot, base + 1 : base + 2, :]


SPLIT = 4
PART = 64
TAIL = 16
HALF = 168
BLOCK = 336


def vmem():
    return pl.BlockSpec(memory_space=pltpu.VMEM)


def shape(*s):
    return jax.ShapeDtypeStruct(s, jnp.float32)


def local(kernel, outs, at, plain, limit, far=(), far_outs=(), scratch=()):
    anywhere = pl.BlockSpec(memory_space=pltpu.MemorySpace.HBM)
    return pl.pallas_call(
        kernel,
        out_shape=list(outs) + list(far_outs),
        in_specs=[pl.BlockSpec(memory_space=pltpu.SMEM)] + [vmem() for _ in plain] + [anywhere for _ in far],
        out_specs=[vmem() for _ in outs] + [anywhere for _ in far_outs],
        scratch_shapes=list(scratch),
        compiler_params=pltpu.CompilerParams(vmem_limit_bytes=limit * 1024 * 1024),
    )(at, *plain, *far)


def offsets(n):
    return [n // 2] + [d for k in range(1, n // 2) for d in (k, -k)] if n > 2 else [1]


def shift(v, axis, d, n):
    return lax.ppermute(v, axis, [(i, (i + d) % n) for i in range(n)])


def gather(v, axis, n):
    me = lax.axis_index(axis)
    out = jnp.zeros((n,) + v.shape, v.dtype)
    out = lax.dynamic_update_index_in_dim(out, v, me, 0)
    for d in offsets(n):
        out = lax.dynamic_update_index_in_dim(out, shift(v, axis, d, n), (me - d) % n, 0)
    return out


def scatter_sum(v, axis, n):
    me = lax.axis_index(axis)
    blocks = v.reshape((n, v.shape[0] // n) + v.shape[1:])
    total = lax.dynamic_index_in_dim(blocks, me, 0, False)
    for d in offsets(n):
        total = total + shift(lax.dynamic_index_in_dim(blocks, (me + d) % n, 0, False), axis, d, n)
    return total


def everyone(v, axes, n):
    return lax.all_to_all(jnp.broadcast_to(v[None], (n,) + v.shape), axes, 0, 0, tiled=False)


def shards(walkers, nuclei, w_embed, w_query, w_key, w_value, w_attn_out, w_mlp, b_mlp, w_out):
    nx, ny, nz = lax.axis_size("x"), lax.axis_size("yh"), lax.axis_size("z")
    groups = lax.axis_size("ylo") * lax.axis_size("core")
    walker_count = nx * ny * nz
    xi, yh = lax.axis_index("x"), lax.axis_index("yh")
    state = lax.axis_index("ylo") * lax.axis_size("core") + lax.axis_index("core")
    states = 2 * groups
    net = state * 2 + yh
    near = ("ylo", "core", "yh")
    gathered = everyone(walkers.reshape(2, 126), near, groups * ny)
    walk = gathered.reshape(groups, ny, 2, 126).transpose(0, 2, 1, 3).reshape(states * ny, 126)
    nuc = jnp.repeat(nuclei.T, 4, axis=1)
    at = yh.reshape(1).astype(jnp.int32)
    mats = (w_query, w_key, w_value, w_attn_out, w_mlp)
    wout = w_out[:, None, :]
    count = states * ny
    total = count * ROWS
    saved = [shape(total, 128)] + [shape(total, D)] * 4 + [shape(total, HEADS * ROWS)] + [shape(total, D)] * 3
    rooms = [pltpu.VMEM(a.shape, jnp.float32) for a in saved]
    la, h2, *kept = local(
        forward_kernel, [shape(count, 128), shape(count, D)], at, (walk, nuc, b_mlp, wout), 61,
        (w_embed,) + mats, saved,
        [pltpu.VMEM((FEAT, D), jnp.float32), pltpu.VMEM((5, D, D), jnp.float32)]
        + rooms
        + [pltpu.SemaphoreType.DMA((6,)), pltpu.SemaphoreType.DMA((9,))],
    )

    logs = everyone(la[:, 0], near, groups * ny).reshape(states, states, ny)
    home = jnp.diagonal(logs, axis1=0, axis2=1).T
    ratios = jnp.exp(logs - home[None])
    part = jnp.sum(ratios, axis=2).T
    sums = jnp.sum(everyone(part, ("x", "z"), nx * nz), axis=0)
    margins = sums / walker_count
    identity = jnp.eye(states, dtype=jnp.float32)
    coupling = margins.T * (1.0 - identity)
    denominator = jnp.sum(coupling[:, :, None] * ratios.transpose(1, 0, 2), axis=1) / walker_count
    cot = coupling.T[:, :, None] * ratios / walker_count - identity[:, :, None] * denominator[None]
    own = lax.dynamic_index_in_dim(cot, net, 0, False).reshape(count)
    own = jnp.broadcast_to(own[:, None], (count, 128))

    place = jnp.stack([xi, yh]).astype(jnp.int32)
    pieces = local(
        backward_kernel, [shape(BLOCK, D)] * 4, place, (own, h2, wout), 61,
        tuple(kept) + mats, (),
        [pltpu.VMEM((5, D, D), jnp.float32)]
        + rooms
        + [pltpu.VMEM((total, D), jnp.float32), pltpu.VMEM((total, 3 * D), jnp.float32),
           pltpu.VMEM((SPLIT, BLOCK, D), jnp.float32), pltpu.SemaphoreType.DMA((14,))],
    )
    mine = pieces[0]
    for d, piece in zip((2, 1, -1), pieces[1:]):
        mine = mine + shift(piece, "x", d, nx)
    mine = jnp.sum(
        lax.all_to_all(mine.reshape(nz, BLOCK // nz, D), "z", 0, 0, tiled=False), axis=0
    )
    mine = everyone(mine, "z", nz).reshape(BLOCK, D)
    a, c = mine[:HALF], mine[HALF:]
    a_far = shift(a, "yh", 1, ny)
    c_far = [shift(c, "x", d, nx) for d in (2, 1, -1)]
    a_far, *c_far = lax.optimization_barrier((a_far, *c_far))
    a = jnp.stack([a, a_far])
    c = jnp.stack([c, *c_far])
    arrays = [a] + [shift(a, "x", d, nx) for d in (2, 1, -1)] + [c, shift(c, "yh", 1, ny)]
    mat = shape(2, D, D)
    mlp, attn, query, key, value, embed, bias, out = local(
        assemble_kernel, [mat] * 5 + [shape(2, FEAT, D), shape(2, 1, D), shape(2, 1, D)],
        place, arrays, 4,
    )
    return (
        margins, embed, query[:, None], key[:, None], value[:, None],
        attn[:, None], mlp[:, None], bias, out[:, 0],
    )


def solution(mesh):
    fine = Mesh(mesh.devices.reshape(2, 2, 4, 2, 8), ("ylo", "core", "x", "yh", "z"))
    s, w = ("ylo", "core"), ("x", "yh", "z")
    return jax.shard_map(
        shards,
        mesh=fine,
        in_specs=(P(s, w, None), P()) + (P(s),) * 8,
        out_specs=(P(),) + (P(s),) * 8,
        check_vma=False,
    )
```

```python
import jax
import jax.numpy as jnp
from jax import lax
from jax.experimental import pallas as pl
from jax.experimental.pallas import tpu as pltpu
from jax.sharding import Mesh, PartitionSpec as P

HEADS = 4
NE = 42
ROWS = 48
D = 256
FEAT = 48
EPS = 1e-05
HIGHEST = lax.Precision.HIGHEST
NN = (((1,), (0,)), ((), ()))
NT = (((1,), (1,)), ((), ()))
TN = (((0,), (0,)), ((), ()))
UNROLL = 4


def exact(a, b, dims):
    return lax.dot_general(a, b, dims, precision=HIGHEST, preferred_element_type=jnp.float32)


def halves(a):
    high = a.astype(jnp.bfloat16)
    return high, (a - high.astype(jnp.float32)).astype(jnp.bfloat16)


def three(a, b, dims):
    def one(x, y):
        return lax.dot_general(x, y, dims, preferred_element_type=jnp.float32)

    return one(a[0], b[0]) + (one(a[0], b[1]) + one(a[1], b[0]))


def stacked_tn(a, b):
    left = jnp.concatenate([a[0], a[0], a[1]], axis=0)
    right = jnp.concatenate([b[0], b[1], b[0]], axis=0)
    return lax.dot_general(left, right, TN, preferred_element_type=jnp.float32)


def normalise(hidden):
    centre = hidden - jnp.mean(hidden, axis=-1, keepdims=True)
    scale = lax.rsqrt(jnp.mean(centre * centre, axis=-1, keepdims=True) + EPS)
    return centre * scale, scale


def normalise_back(grad, normed, scale):
    return scale * (
        grad
        - jnp.mean(grad, axis=-1, keepdims=True)
        - normed * jnp.mean(grad * normed, axis=-1, keepdims=True)
    )


def head_masks():
    lane = lax.broadcasted_iota(jnp.int32, (1, D), 1)
    return [(lane // (D // HEADS)) == h for h in range(HEADS)]


def spread(block, masks):
    return jnp.concatenate([jnp.where(m, block, 0.0) for m in masks], axis=0)


def gather_heads(stacked, masks):
    out = jnp.where(masks[0], stacked[:ROWS], 0.0)
    for h in range(1, HEADS):
        out = out + jnp.where(masks[h], stacked[h * ROWS : (h + 1) * ROWS], 0.0)
    return out


def fetch(source, target, sem):
    copy = pltpu.make_async_copy(source, target, sem)
    copy.start()
    return copy


def piece(source, target, step, sem):
    size = UNROLL * ROWS
    rows = pl.ds(step * size, size)
    if not isinstance(step, int):
        rows = pl.ds(pl.multiple_of(step * size, size), size)
    return pltpu.make_async_copy(source.at[rows], target.at[rows], sem)


def forward_kernel(
    net_ref, walk_ref, nuc_ref, b_ref, wout_ref, we_hbm, wq_hbm, wk_hbm, wv_hbm, wo_hbm, wm_hbm,
    la_ref, h2_ref, feat_hbm, x_hbm, q_hbm, k_hbm, v_hbm, at_hbm, mix_hbm, h1_hbm,
    we_ref, w_ref, feat_ref, x_ref, q_ref, k_ref, v_ref, at_ref, mix_ref, h1_ref, in_sem, out_sem,
):
    at = net_ref[0]
    loads = [fetch(we_hbm.at[at], we_ref, in_sem.at[0])]
    for i, w in enumerate((wq_hbm, wk_hbm, wv_hbm, wo_hbm, wm_hbm)):
        loads.append(fetch(w.at[at, 0], w_ref.at[i], in_sem.at[1 + i]))
    count = walk_ref.shape[0]
    width = walk_ref.shape[1]
    electron = lax.broadcasted_iota(jnp.int32, (ROWS, width), 0)
    lane = lax.broadcasted_iota(jnp.int32, (ROWS, width), 1)
    picks = [lane == 3 * electron + c for c in range(3)]
    flane = lax.broadcasted_iota(jnp.int32, (1, FEAT), 1)
    kind = flane % 4
    masks = head_masks()
    n = [nuc_ref[c : c + 1, :] for c in range(3)]
    for w in range(count):
        row = jnp.broadcast_to(walk_ref[w : w + 1, :], (ROWS, width))
        off = [
            jnp.sum(jnp.where(picks[c], row, 0.0), axis=1, keepdims=True) - n[c] for c in range(3)
        ]
        dist = jnp.sqrt(off[0] * off[0] + off[1] * off[1] + off[2] * off[2] + 1.0)
        feat = jnp.where(kind == 0, off[0], jnp.where(kind == 1, off[1], jnp.where(kind == 2, off[2], dist)))
        feat_ref[w * ROWS : (w + 1) * ROWS, :FEAT] = feat
    loads[0].wait()
    h0 = exact(feat_ref[:, :FEAT], we_ref[...], NN)
    x, r1 = normalise(h0)
    feat_ref[:, FEAT : FEAT + 1] = r1
    x_ref[...] = x
    stores = [fetch(x_ref, x_hbm, out_sem.at[0]), fetch(feat_ref, feat_hbm, out_sem.at[4])]
    loads[1].wait()
    q_ref[...] = exact(x, w_ref[0], NN) * 0.125
    stores.append(fetch(q_ref, q_hbm, out_sem.at[1]))
    loads[2].wait()
    k_ref[...] = exact(x, w_ref[1], NN)
    stores.append(fetch(k_ref, k_hbm, out_sem.at[2]))
    loads[3].wait()
    v_ref[...] = three(halves(x), halves(w_ref[2]), NN)
    stores.append(fetch(v_ref, v_hbm, out_sem.at[3]))
    key_row = lax.broadcasted_iota(jnp.int32, (ROWS, HEADS * ROWS), 0)

    def attend(step, carry):
        spans = [
            pl.ds(pl.multiple_of(step * (UNROLL * ROWS) + u * ROWS, ROWS), ROWS) for u in range(UNROLL)
        ]
        scores = [exact(k_ref[rows, :], spread(q_ref[rows, :], masks), NT) for rows in spans]
        scores = [jnp.where(key_row < NE, a, -1e30) for a in scores]
        weights = [jnp.exp(a - jnp.max(a, axis=0, keepdims=True)) for a in scores]
        attention = [a / jnp.sum(a, axis=0, keepdims=True) for a in weights]
        for rows, a in zip(spans, attention):
            at_ref[rows, :] = a
        mixed = [stacked_tn(halves(a), halves(v_ref[rows, :])) for rows, a in zip(spans, attention)]
        for rows, a in zip(spans, mixed):
            mix_ref[rows, :] = gather_heads(a, masks)
        for i, (a, b) in enumerate(((at_ref, at_hbm), (mix_ref, mix_hbm))):
            piece(a, b, step, out_sem.at[6 + 4 * i + step]).start()
        return carry

    lax.fori_loop(0, count // UNROLL, attend, 0)
    for step in range(count // UNROLL):
        for i, (a, b) in enumerate(((at_ref, at_hbm), (mix_ref, mix_hbm))):
            stores.append(piece(a, b, step, out_sem.at[6 + 4 * i + step]))
    loads[4].wait()
    h1 = h0 + three(halves(mix_ref[...]), halves(w_ref[3]), NN)
    h1_ref[...] = h1
    stores.append(fetch(h1_ref, h1_hbm, out_sem.at[5]))
    y, _ = normalise(h1)
    loads[5].wait()
    t = jnp.tanh(three(halves(y), halves(w_ref[4]), NN) + b_ref[at])
    h2 = h1 + t
    real = lax.broadcasted_iota(jnp.int32, (ROWS, 1), 0) < NE
    for w in range(count):
        total = jnp.sum(jnp.where(real, h2[w * ROWS : (w + 1) * ROWS, :], 0.0), axis=0, keepdims=True) / NE
        h2_ref[w : w + 1, :] = total
        la_ref[w : w + 1, :] = jnp.broadcast_to(
            jnp.sum(total * wout_ref[at], axis=1, keepdims=True), (1, 128)
        )
    for copy in stores:
        copy.wait()


def backward_kernel(
    where_ref, c_ref, h2_ref, b_ref, wout_ref,
    feat_hbm, x_hbm, q_hbm, k_hbm, v_hbm, at_hbm, mix_hbm, h1_hbm,
    wq_hbm, wk_hbm, wv_hbm, wo_hbm, wm_hbm,
    own_ref, far_ref, up_ref, down_ref,
    w_ref, feat_ref, x_ref, q_ref, k_ref, v_ref, at_ref, mix_ref, h1_ref,
    do_ref, dqkv_ref, out_ref, sem,
):
    me, at = where_ref[0], where_ref[1]
    count = c_ref.shape[0]
    steps = count // UNROLL
    first = [
        fetch(h1_hbm, h1_ref, sem.at[0]),
        fetch(wm_hbm.at[at, 0], w_ref.at[4], sem.at[1]),
        fetch(wo_hbm.at[at, 0], w_ref.at[3], sem.at[2]),
    ]
    chunked = ((at_hbm, at_ref), (v_hbm, v_ref), (q_hbm, q_ref), (k_hbm, k_ref))
    for step in range(steps):
        for i, (a, b) in enumerate(chunked):
            piece(a, b, step, sem.at[16 + steps * i + step]).start()
    later = (
        (wq_hbm.at[at, 0], w_ref.at[0]), (wk_hbm.at[at, 0], w_ref.at[1]), (wv_hbm.at[at, 0], w_ref.at[2]),
        (x_hbm, x_ref), (feat_hbm, feat_ref), (mix_hbm, mix_ref),
    )
    later = [fetch(a, b, sem.at[3 + i]) for i, (a, b) in enumerate(later)]
    masks = head_masks()
    real = lax.broadcasted_iota(jnp.int32, (ROWS, 1), 0) < NE
    factor = jnp.concatenate(
        [jnp.where(real, c_ref[w : w + 1, :1] / NE, 0.0) for w in range(count)], axis=0
    )

    def put(i, value):
        for block in range(SPLIT):
            out_ref[block, i * PART : (i + 1) * PART, :] = value[block * PART : (block + 1) * PART, :]

    g = factor * wout_ref[at]
    first[0].wait()
    y, r2 = normalise(h1_ref[...])
    y_parts = halves(y)
    first[1].wait()
    wm = halves(w_ref[4])
    t = jnp.tanh(three(y_parts, wm, NN) + b_ref[at])
    dm = g * (1.0 - t * t)
    dm_parts = halves(dm)
    dy = three(dm_parts, wm, NT)
    put(0, three(y_parts, dm_parts, TN))
    dh1 = g + normalise_back(dy, y, r2)
    dh1_parts = halves(dh1)
    first[2].wait()
    do_ref[...] = three(dh1_parts, halves(w_ref[3]), NT)

    def attend(step, carry):
        for i, (a, b) in enumerate(chunked):
            piece(a, b, step, sem.at[16 + steps * i + step]).wait()
        spans = [
            pl.ds(pl.multiple_of(step * (UNROLL * ROWS) + u * ROWS, ROWS), ROWS) for u in range(UNROLL)
        ]
        attention = [at_ref[rows, :] for rows in spans]
        do = [halves(spread(do_ref[rows, :], masks)) for rows in spans]
        da = [three(halves(v_ref[rows, :]), a, NT) for rows, a in zip(spans, do)]
        dv = [three(halves(a), b, NN) for a, b in zip(attention, do)]
        ds = [a * (b - jnp.sum(b * a, axis=0, keepdims=True)) for a, b in zip(attention, da)]
        ds = [halves(a) for a in ds]
        dk = [three(a, halves(spread(q_ref[rows, :], masks)), NN) for rows, a in zip(spans, ds)]
        dq = [stacked_tn(a, halves(k_ref[rows, :])) for rows, a in zip(spans, ds)]
        for rows, a, b, c in zip(spans, dq, dk, dv):
            dqkv_ref[rows, :D] = gather_heads(a, masks) * 0.125
            dqkv_ref[rows, D : 2 * D] = b
            dqkv_ref[rows, 2 * D :] = c
        return carry

    lax.fori_loop(0, steps, attend, 0)
    for copy in later[:5]:
        copy.wait()
    x = x_ref[...]
    x_parts = halves(x)
    dx = None
    for i in range(3):
        part = halves(dqkv_ref[:, i * D : (i + 1) * D])
        term = three(part, halves(w_ref[i]), NT)
        dx = term if dx is None else dx + term
        put(2 + i, three(x_parts, part, TN))
    later[5].wait()
    put(1, three(halves(mix_ref[...]), dh1_parts, TN))
    dh0 = dh1 + normalise_back(dx, x, feat_ref[:, FEAT : FEAT + 1])
    base = 5 * PART
    embed = three(halves(feat_ref[:, :FEAT]), halves(dh0), TN)
    for block in range(SPLIT - 1):
        out_ref[block, base:, :] = embed[block * TAIL : (block + 1) * TAIL, :]
    out_ref[SPLIT - 1, base:, :] = jnp.concatenate(
        [
            jnp.sum(dm, axis=0, keepdims=True),
            jnp.sum(c_ref[:, :1] * h2_ref[...], axis=0, keepdims=True),
            jnp.zeros((TAIL - 2, D), jnp.float32),
        ],
        axis=0,
    )
    for ref, d in ((own_ref, 0), (far_ref, 2), (up_ref, 1), (down_ref, 3)):
        ref[...] = out_ref[(me + d) % SPLIT]


def assemble_kernel(
    where_ref, a0_ref, a1_ref, a2_ref, a3_ref, c0_ref, c1_ref,
    mlp_ref, attn_ref, query_ref, key_ref, value_ref, embed_ref, bias_ref, out_ref,
):
    me, yh = where_ref[0], where_ref[1]
    mats = (mlp_ref, attn_ref, query_ref, key_ref, value_ref)
    for slot, (d, a_ref) in enumerate(((0, a0_ref), (2, a1_ref), (1, a2_ref), (3, a3_ref))):
        block = (me + SPLIT - d) % SPLIT
        start = pl.multiple_of(block * PART, PART)
        for pair, c_ref in enumerate((c0_ref, c1_ref)):
            net = yh if pair == 0 else 1 - yh
            for i in range(5):
                low, high = i * PART, (i + 1) * PART
                cut = min(max(low, HALF), high)
                if cut > low:
                    mats[i][net, pl.ds(start, cut - low), :] = a_ref[pair, low:cut, :]
                if high > cut:
                    mats[i][net, pl.ds(pl.multiple_of(start + (cut - low), 8), high - cut), :] = c_ref[
                        slot, cut - HALF : high - HALF, :
                    ]
            base = 5 * PART - HALF

            @pl.when(block < SPLIT - 1)
            def _():
                embed_ref[net, pl.ds(pl.multiple_of(block * TAIL, TAIL), TAIL), :] = c_ref[slot, base:, :]

            @pl.when(block == SPLIT - 1)
            def _():
                bias_ref[net] = c_ref[slot, base : base + 1, :]
                out_ref[net] = c_ref[slot, base + 1 : base + 2, :]


SPLIT = 4
PART = 64
TAIL = 16
HALF = 168
BLOCK = 336


def vmem():
    return pl.BlockSpec(memory_space=pltpu.VMEM)


def shape(*s):
    return jax.ShapeDtypeStruct(s, jnp.float32)


def local(kernel, outs, at, plain, limit, far=(), far_outs=(), scratch=()):
    anywhere = pl.BlockSpec(memory_space=pltpu.MemorySpace.HBM)
    return pl.pallas_call(
        kernel,
        out_shape=list(outs) + list(far_outs),
        in_specs=[pl.BlockSpec(memory_space=pltpu.SMEM)] + [vmem() for _ in plain] + [anywhere for _ in far],
        out_specs=[vmem() for _ in outs] + [anywhere for _ in far_outs],
        scratch_shapes=list(scratch),
        compiler_params=pltpu.CompilerParams(vmem_limit_bytes=limit * 1024 * 1024),
    )(at, *plain, *far)


def offsets(n):
    return [n // 2] + [d for k in range(1, n // 2) for d in (k, -k)] if n > 2 else [1]


def shift(v, axis, d, n):
    return lax.ppermute(v, axis, [(i, (i + d) % n) for i in range(n)])


def gather(v, axis, n):
    me = lax.axis_index(axis)
    out = jnp.zeros((n,) + v.shape, v.dtype)
    out = lax.dynamic_update_index_in_dim(out, v, me, 0)
    for d in offsets(n):
        out = lax.dynamic_update_index_in_dim(out, shift(v, axis, d, n), (me - d) % n, 0)
    return out


def scatter_sum(v, axis, n):
    me = lax.axis_index(axis)
    blocks = v.reshape((n, v.shape[0] // n) + v.shape[1:])
    total = lax.dynamic_index_in_dim(blocks, me, 0, False)
    for d in offsets(n):
        total = total + shift(lax.dynamic_index_in_dim(blocks, (me + d) % n, 0, False), axis, d, n)
    return total


def everyone(v, axes, n):
    return lax.all_to_all(jnp.broadcast_to(v[None], (n,) + v.shape), axes, 0, 0, tiled=False)


def shards(walkers, nuclei, w_embed, w_query, w_key, w_value, w_attn_out, w_mlp, b_mlp, w_out):
    nx, ny, nz = lax.axis_size("x"), lax.axis_size("yh"), lax.axis_size("z")
    groups = lax.axis_size("ylo") * lax.axis_size("core")
    walker_count = nx * ny * nz
    xi, yh = lax.axis_index("x"), lax.axis_index("yh")
    state = lax.axis_index("ylo") * lax.axis_size("core") + lax.axis_index("core")
    states = 2 * groups
    net = state * 2 + yh
    near = ("ylo", "core", "yh")
    gathered = everyone(walkers.reshape(2, 126), near, groups * ny)
    walk = gathered.reshape(groups, ny, 2, 126).transpose(0, 2, 1, 3).reshape(states * ny, 126)
    nuc = jnp.repeat(nuclei.T, 4, axis=1)
    at = yh.reshape(1).astype(jnp.int32)
    mats = (w_query, w_key, w_value, w_attn_out, w_mlp)
    wout = w_out[:, None, :]
    count = states * ny
    total = count * ROWS
    saved = [shape(total, 128)] + [shape(total, D)] * 4 + [shape(total, HEADS * ROWS)] + [shape(total, D)] * 2
    rooms = [pltpu.VMEM(a.shape, jnp.float32) for a in saved]
    la, h2, *kept = local(
        forward_kernel, [shape(count, 128), shape(count, D)], at, (walk, nuc, b_mlp, wout), 61,
        (w_embed,) + mats, saved,
        [pltpu.VMEM((FEAT, D), jnp.float32), pltpu.VMEM((5, D, D), jnp.float32)]
        + rooms
        + [pltpu.SemaphoreType.DMA((6,)), pltpu.SemaphoreType.DMA((14,))],
    )

    logs = everyone(la[:, 0], near, groups * ny).reshape(states, states, ny)
    home = jnp.diagonal(logs, axis1=0, axis2=1).T
    ratios = jnp.exp(logs - home[None])
    part = jnp.sum(ratios, axis=2).T
    sums = jnp.sum(everyone(part, ("x", "z"), nx * nz), axis=0)
    margins = sums / walker_count
    identity = jnp.eye(states, dtype=jnp.float32)
    coupling = margins.T * (1.0 - identity)
    denominator = jnp.sum(coupling[:, :, None] * ratios.transpose(1, 0, 2), axis=1) / walker_count
    cot = coupling.T[:, :, None] * ratios / walker_count - identity[:, :, None] * denominator[None]
    own = lax.dynamic_index_in_dim(cot, net, 0, False).reshape(count)
    own = jnp.broadcast_to(own[:, None], (count, 128))

    place = jnp.stack([xi, yh]).astype(jnp.int32)
    pieces = local(
        backward_kernel, [shape(BLOCK, D)] * 4, place, (own, h2, b_mlp, wout), 61,
        tuple(kept) + mats, (),
        [pltpu.VMEM((5, D, D), jnp.float32)]
        + rooms
        + [pltpu.VMEM((total, D), jnp.float32), pltpu.VMEM((total, 3 * D), jnp.float32),
           pltpu.VMEM((SPLIT, BLOCK, D), jnp.float32), pltpu.SemaphoreType.DMA((32,))],
    )
    mine = pieces[0]
    for d, piece in zip((2, 1, -1), pieces[1:]):
        mine = mine + shift(piece, "x", d, nx)
    mine = jnp.sum(
        lax.all_to_all(mine.reshape(nz, BLOCK // nz, D), "z", 0, 0, tiled=False), axis=0
    )
    mine = everyone(mine, "z", nz).reshape(BLOCK, D)
    a, c = mine[:HALF], mine[HALF:]
    a_far = shift(a, "yh", 1, ny)
    c_far = [shift(c, "x", d, nx) for d in (2, 1, -1)]
    a_far, *c_far = lax.optimization_barrier((a_far, *c_far))
    a = jnp.stack([a, a_far])
    c = jnp.stack([c, *c_far])
    arrays = [a] + [shift(a, "x", d, nx) for d in (2, 1, -1)] + [c, shift(c, "yh", 1, ny)]
    mat = shape(2, D, D)
    mlp, attn, query, key, value, embed, bias, out = local(
        assemble_kernel, [mat] * 5 + [shape(2, FEAT, D), shape(2, 1, D), shape(2, 1, D)],
        place, arrays, 4,
    )
    return (
        margins, embed, query[:, None], key[:, None], value[:, None],
        attn[:, None], mlp[:, None], bias, out[:, 0],
    )


def solution(mesh):
    fine = Mesh(mesh.devices.reshape(2, 2, 4, 2, 8), ("ylo", "core", "x", "yh", "z"))
    s, w = ("ylo", "core"), ("x", "yh", "z")
    return jax.shard_map(
        shards,
        mesh=fine,
        in_specs=(P(s, w, None), P()) + (P(s),) * 8,
        out_specs=(P(),) + (P(s),) * 8,
        check_vma=False,
    )
```

```python
import jax
import jax.numpy as jnp
from jax import lax
from jax.experimental import pallas as pl
from jax.experimental.pallas import tpu as pltpu
from jax.sharding import Mesh, PartitionSpec as P

HEADS = 4
NE = 42
ROWS = 48
D = 256
FEAT = 48
EPS = 1e-05
HIGHEST = lax.Precision.HIGHEST
NN = (((1,), (0,)), ((), ()))
NT = (((1,), (1,)), ((), ()))
TN = (((0,), (0,)), ((), ()))
UNROLL = 4


def exact(a, b, dims):
    return lax.dot_general(a, b, dims, precision=HIGHEST, preferred_element_type=jnp.float32)


def halves(a):
    high = a.astype(jnp.bfloat16)
    return high, (a - high.astype(jnp.float32)).astype(jnp.bfloat16)


def three(a, b, dims):
    def one(x, y):
        return lax.dot_general(x, y, dims, preferred_element_type=jnp.float32)

    return one(a[0], b[0]) + (one(a[0], b[1]) + one(a[1], b[0]))


def stacked_tn(a, b):
    left = jnp.concatenate([a[0], a[0], a[1]], axis=0)
    right = jnp.concatenate([b[0], b[1], b[0]], axis=0)
    return lax.dot_general(left, right, TN, preferred_element_type=jnp.float32)


def normalise(hidden):
    centre = hidden - jnp.mean(hidden, axis=-1, keepdims=True)
    scale = lax.rsqrt(jnp.mean(centre * centre, axis=-1, keepdims=True) + EPS)
    return centre * scale, scale


def normalise_back(grad, normed, scale):
    return scale * (
        grad
        - jnp.mean(grad, axis=-1, keepdims=True)
        - normed * jnp.mean(grad * normed, axis=-1, keepdims=True)
    )


def head_masks():
    lane = lax.broadcasted_iota(jnp.int32, (1, D), 1)
    return [(lane // (D // HEADS)) == h for h in range(HEADS)]


def spread(block, masks):
    return jnp.concatenate([jnp.where(m, block, 0.0) for m in masks], axis=0)


def gather_heads(stacked, masks):
    out = jnp.where(masks[0], stacked[:ROWS], 0.0)
    for h in range(1, HEADS):
        out = out + jnp.where(masks[h], stacked[h * ROWS : (h + 1) * ROWS], 0.0)
    return out


def fetch(source, target, sem):
    copy = pltpu.make_async_copy(source, target, sem)
    copy.start()
    return copy


def piece(source, target, step, sem):
    size = UNROLL * ROWS
    rows = pl.ds(step * size, size)
    if not isinstance(step, int):
        rows = pl.ds(pl.multiple_of(step * size, size), size)
    return pltpu.make_async_copy(source.at[rows], target.at[rows], sem)


def forward_kernel(
    net_ref, walk_ref, nuc_ref, b_ref, wout_ref, we_hbm, wq_hbm, wk_hbm, wv_hbm, wo_hbm, wm_hbm,
    la_ref, h2_ref, feat_hbm, x_hbm, q_hbm, k_hbm, v_hbm, at_hbm, mix_hbm, h1_hbm,
    we_ref, w_ref, feat_ref, x_ref, q_ref, k_ref, v_ref, at_ref, mix_ref, h1_ref, in_sem, out_sem,
):
    at = net_ref[0]
    loads = [fetch(we_hbm.at[at], we_ref, in_sem.at[0])]
    for i, w in enumerate((wq_hbm, wk_hbm, wv_hbm, wo_hbm, wm_hbm)):
        loads.append(fetch(w.at[at, 0], w_ref.at[i], in_sem.at[1 + i]))
    count = walk_ref.shape[0]
    width = walk_ref.shape[1]
    electron = lax.broadcasted_iota(jnp.int32, (ROWS, width), 0)
    lane = lax.broadcasted_iota(jnp.int32, (ROWS, width), 1)
    picks = [lane == 3 * electron + c for c in range(3)]
    flane = lax.broadcasted_iota(jnp.int32, (1, FEAT), 1)
    kind = flane % 4
    masks = head_masks()
    n = [nuc_ref[c : c + 1, :] for c in range(3)]
    for w in range(count):
        row = jnp.broadcast_to(walk_ref[w : w + 1, :], (ROWS, width))
        off = [
            jnp.sum(jnp.where(picks[c], row, 0.0), axis=1, keepdims=True) - n[c] for c in range(3)
        ]
        dist = jnp.sqrt(off[0] * off[0] + off[1] * off[1] + off[2] * off[2] + 1.0)
        feat = jnp.where(kind == 0, off[0], jnp.where(kind == 1, off[1], jnp.where(kind == 2, off[2], dist)))
        feat_ref[w * ROWS : (w + 1) * ROWS, :FEAT] = feat
    loads[0].wait()
    h0 = exact(feat_ref[:, :FEAT], we_ref[...], NN)
    x, r1 = normalise(h0)
    feat_ref[:, FEAT : FEAT + 1] = r1
    x_ref[...] = x
    stores = [fetch(x_ref, x_hbm, out_sem.at[0]), fetch(feat_ref, feat_hbm, out_sem.at[4])]
    loads[1].wait()
    q_ref[...] = exact(x, w_ref[0], NN) * 0.125
    stores.append(fetch(q_ref, q_hbm, out_sem.at[1]))
    loads[2].wait()
    k_ref[...] = exact(x, w_ref[1], NN)
    stores.append(fetch(k_ref, k_hbm, out_sem.at[2]))
    loads[3].wait()
    v_ref[...] = three(halves(x), halves(w_ref[2]), NN)
    stores.append(fetch(v_ref, v_hbm, out_sem.at[3]))
    key_row = lax.broadcasted_iota(jnp.int32, (ROWS, HEADS * ROWS), 0)

    def attend(step, carry):
        spans = [
            pl.ds(pl.multiple_of(step * (UNROLL * ROWS) + u * ROWS, ROWS), ROWS) for u in range(UNROLL)
        ]
        scores = [exact(k_ref[rows, :], spread(q_ref[rows, :], masks), NT) for rows in spans]
        scores = [jnp.where(key_row < NE, a, -1e30) for a in scores]
        weights = [jnp.exp(a - jnp.max(a, axis=0, keepdims=True)) for a in scores]
        attention = [a / jnp.sum(a, axis=0, keepdims=True) for a in weights]
        for rows, a in zip(spans, attention):
            at_ref[rows, :] = a
        mixed = [stacked_tn(halves(a), halves(v_ref[rows, :])) for rows, a in zip(spans, attention)]
        for rows, a in zip(spans, mixed):
            mix_ref[rows, :] = gather_heads(a, masks)
        for i, (a, b) in enumerate(((at_ref, at_hbm), (mix_ref, mix_hbm))):
            piece(a, b, step, out_sem.at[6 + 4 * i + step]).start()
        return carry

    lax.fori_loop(0, count // UNROLL, attend, 0)
    for step in range(count // UNROLL):
        for i, (a, b) in enumerate(((at_ref, at_hbm), (mix_ref, mix_hbm))):
            stores.append(piece(a, b, step, out_sem.at[6 + 4 * i + step]))
    loads[4].wait()
    h1 = h0 + three(halves(mix_ref[...]), halves(w_ref[3]), NN)
    h1_ref[...] = h1
    stores.append(fetch(h1_ref, h1_hbm, out_sem.at[5]))
    y, _ = normalise(h1)
    loads[5].wait()
    t = jnp.tanh(three(halves(y), halves(w_ref[4]), NN) + b_ref[at])
    h2 = h1 + t
    real = lax.broadcasted_iota(jnp.int32, (ROWS, 1), 0) < NE
    for w in range(count):
        total = jnp.sum(jnp.where(real, h2[w * ROWS : (w + 1) * ROWS, :], 0.0), axis=0, keepdims=True) / NE
        h2_ref[w : w + 1, :] = total
        la_ref[w : w + 1, :] = jnp.broadcast_to(
            jnp.sum(total * wout_ref[at], axis=1, keepdims=True), (1, 128)
        )
    for copy in stores:
        copy.wait()


def backward_kernel(
    where_ref, c_ref, h2_ref, b_ref, wout_ref,
    feat_hbm, x_hbm, q_hbm, k_hbm, v_hbm, at_hbm, mix_hbm, h1_hbm,
    wq_hbm, wk_hbm, wv_hbm, wo_hbm, wm_hbm,
    own_ref, far_ref, up_ref, down_ref,
    w_ref, feat_ref, x_ref, q_ref, k_ref, v_ref, at_ref, mix_ref, h1_ref,
    do_ref, dqkv_ref, out_ref, sem,
):
    me, at = where_ref[0], where_ref[1]
    count = c_ref.shape[0]
    steps = count // UNROLL
    first = [
        fetch(h1_hbm, h1_ref, sem.at[0]),
        fetch(wm_hbm.at[at, 0], w_ref.at[4], sem.at[1]),
        fetch(wo_hbm.at[at, 0], w_ref.at[3], sem.at[2]),
    ]
    chunked = ((at_hbm, at_ref), (v_hbm, v_ref), (q_hbm, q_ref), (k_hbm, k_ref))
    for step in range(steps):
        for i, (a, b) in enumerate(chunked):
            piece(a, b, step, sem.at[16 + steps * i + step]).start()
    later = (
        (wq_hbm.at[at, 0], w_ref.at[0]), (wk_hbm.at[at, 0], w_ref.at[1]), (wv_hbm.at[at, 0], w_ref.at[2]),
        (x_hbm, x_ref), (feat_hbm, feat_ref), (mix_hbm, mix_ref),
    )
    later = [fetch(a, b, sem.at[3 + i]) for i, (a, b) in enumerate(later)]
    masks = head_masks()
    real = lax.broadcasted_iota(jnp.int32, (ROWS, 1), 0) < NE
    factor = jnp.concatenate(
        [jnp.where(real, c_ref[w : w + 1, :1] / NE, 0.0) for w in range(count)], axis=0
    )

    def put(i, value):
        for block in range(SPLIT):
            out_ref[block, i * PART : (i + 1) * PART, :] = value[block * PART : (block + 1) * PART, :]

    g = factor * wout_ref[at]
    first[0].wait()
    y, r2 = normalise(h1_ref[...])
    y_parts = halves(y)
    first[1].wait()
    wm = halves(w_ref[4])
    t = jnp.tanh(three(y_parts, wm, NN) + b_ref[at])
    dm = g * (1.0 - t * t)
    dm_parts = halves(dm)
    dy = three(dm_parts, wm, NT)
    put(0, three(y_parts, dm_parts, TN))
    dh1 = g + normalise_back(dy, y, r2)
    dh1_parts = halves(dh1)
    first[2].wait()
    do_ref[...] = three(dh1_parts, halves(w_ref[3]), NT)

    def attend(step, carry):
        for i, (a, b) in enumerate(chunked):
            piece(a, b, step, sem.at[16 + steps * i + step]).wait()
        spans = [
            pl.ds(pl.multiple_of(step * (UNROLL * ROWS) + u * ROWS, ROWS), ROWS) for u in range(UNROLL)
        ]
        attention = [at_ref[rows, :] for rows in spans]
        do = [halves(spread(do_ref[rows, :], masks)) for rows in spans]
        da = [three(halves(v_ref[rows, :]), a, NT) for rows, a in zip(spans, do)]
        dv = [three(halves(a), b, NN) for a, b in zip(attention, do)]
        ds = [a * (b - jnp.sum(b * a, axis=0, keepdims=True)) for a, b in zip(attention, da)]
        ds = [halves(a) for a in ds]
        dk = [three(a, halves(spread(q_ref[rows, :], masks)), NN) for rows, a in zip(spans, ds)]
        dq = [stacked_tn(a, halves(k_ref[rows, :])) for rows, a in zip(spans, ds)]
        for rows, a, b, c in zip(spans, dq, dk, dv):
            dqkv_ref[rows, :D] = gather_heads(a, masks) * 0.125
            dqkv_ref[rows, D : 2 * D] = b
            dqkv_ref[rows, 2 * D :] = c
        return carry

    lax.fori_loop(0, steps, attend, 0)
    for copy in later[:5]:
        copy.wait()
    x = x_ref[...]
    x_parts = halves(x)
    dx = None
    for i in range(3):
        part = halves(dqkv_ref[:, i * D : (i + 1) * D])
        term = three(part, halves(w_ref[i]), NT)
        dx = term if dx is None else dx + term
        put(2 + i, three(x_parts, part, TN))
    later[5].wait()
    put(1, three(halves(mix_ref[...]), dh1_parts, TN))
    dh0 = dh1 + normalise_back(dx, x, feat_ref[:, FEAT : FEAT + 1])
    base = 5 * PART
    embed = three(halves(feat_ref[:, :FEAT]), halves(dh0), TN)
    for block in range(SPLIT - 1):
        out_ref[block, base:, :] = embed[block * TAIL : (block + 1) * TAIL, :]
    out_ref[SPLIT - 1, base:, :] = jnp.concatenate(
        [
            jnp.sum(dm, axis=0, keepdims=True),
            jnp.sum(c_ref[:, :1] * h2_ref[...], axis=0, keepdims=True),
            jnp.zeros((TAIL - 2, D), jnp.float32),
        ],
        axis=0,
    )
    for ref, d in ((own_ref, 0), (far_ref, 2), (up_ref, 1), (down_ref, 3)):
        ref[...] = out_ref[(me + d) % SPLIT]


def assemble_kernel(
    where_ref, a0_ref, a1_ref, a2_ref, a3_ref, c0_ref, c1_ref,
    mlp_ref, attn_ref, query_ref, key_ref, value_ref, embed_ref, bias_ref, out_ref,
):
    me, yh = where_ref[0], where_ref[1]
    mats = (mlp_ref, attn_ref, query_ref, key_ref, value_ref)
    for slot, (d, a_ref) in enumerate(((0, a0_ref), (2, a1_ref), (1, a2_ref), (3, a3_ref))):
        block = (me + SPLIT - d) % SPLIT
        start = pl.multiple_of(block * PART, PART)
        for pair, c_ref in enumerate((c0_ref, c1_ref)):
            net = yh if pair == 0 else 1 - yh
            for i in range(5):
                low, high = i * PART, (i + 1) * PART
                cut = min(max(low, HALF), high)
                if cut > low:
                    mats[i][net, pl.ds(start, cut - low), :] = a_ref[pair, low:cut, :]
                if high > cut:
                    mats[i][net, pl.ds(pl.multiple_of(start + (cut - low), 8), high - cut), :] = c_ref[
                        slot, cut - HALF : high - HALF, :
                    ]
            base = 5 * PART - HALF

            @pl.when(block < SPLIT - 1)
            def _():
                embed_ref[net, pl.ds(pl.multiple_of(block * TAIL, TAIL), TAIL), :] = c_ref[slot, base:, :]

            @pl.when(block == SPLIT - 1)
            def _():
                bias_ref[net] = c_ref[slot, base : base + 1, :]
                out_ref[net] = c_ref[slot, base + 1 : base + 2, :]


SPLIT = 4
PART = 64
TAIL = 16
HALF = 168
BLOCK = 336


def vmem():
    return pl.BlockSpec(memory_space=pltpu.VMEM)


def shape(*s):
    return jax.ShapeDtypeStruct(s, jnp.float32)


def local(kernel, outs, at, plain, limit, far=(), far_outs=(), scratch=()):
    anywhere = pl.BlockSpec(memory_space=pltpu.MemorySpace.HBM)
    return pl.pallas_call(
        kernel,
        out_shape=list(outs) + list(far_outs),
        in_specs=[pl.BlockSpec(memory_space=pltpu.SMEM)] + [vmem() for _ in plain] + [anywhere for _ in far],
        out_specs=[vmem() for _ in outs] + [anywhere for _ in far_outs],
        scratch_shapes=list(scratch),
        compiler_params=pltpu.CompilerParams(vmem_limit_bytes=limit * 1024 * 1024),
    )(at, *plain, *far)


def offsets(n):
    return [n // 2] + [d for k in range(1, n // 2) for d in (k, -k)] if n > 2 else [1]


def shift(v, axis, d, n):
    return lax.ppermute(v, axis, [(i, (i + d) % n) for i in range(n)])


def gather(v, axis, n):
    me = lax.axis_index(axis)
    out = jnp.zeros((n,) + v.shape, v.dtype)
    out = lax.dynamic_update_index_in_dim(out, v, me, 0)
    for d in offsets(n):
        out = lax.dynamic_update_index_in_dim(out, shift(v, axis, d, n), (me - d) % n, 0)
    return out


def scatter_sum(v, axis, n):
    me = lax.axis_index(axis)
    blocks = v.reshape((n, v.shape[0] // n) + v.shape[1:])
    total = lax.dynamic_index_in_dim(blocks, me, 0, False)
    for d in offsets(n):
        total = total + shift(lax.dynamic_index_in_dim(blocks, (me + d) % n, 0, False), axis, d, n)
    return total


def everyone(v, axes, n):
    return lax.all_to_all(jnp.broadcast_to(v[None], (n,) + v.shape), axes, 0, 0, tiled=False)


def shards(walkers, nuclei, w_embed, w_query, w_key, w_value, w_attn_out, w_mlp, b_mlp, w_out):
    nx, ny, nz = lax.axis_size("x"), lax.axis_size("yh"), lax.axis_size("z")
    groups = lax.axis_size("ylo") * lax.axis_size("core")
    walker_count = nx * ny * nz
    xi, yh = lax.axis_index("x"), lax.axis_index("yh")
    state = lax.axis_index("ylo") * lax.axis_size("core") + lax.axis_index("core")
    states = 2 * groups
    net = state * 2 + yh
    near = ("ylo", "core", "yh")
    gathered = everyone(walkers.reshape(2, 126), near, groups * ny)
    walk = gathered.reshape(groups, ny, 2, 126).transpose(0, 2, 1, 3).reshape(states * ny, 126)
    nuc = jnp.repeat(nuclei.T, 4, axis=1)
    at = yh.reshape(1).astype(jnp.int32)
    mats = (w_query, w_key, w_value, w_attn_out, w_mlp)
    wout = w_out[:, None, :]
    count = states * ny
    total = count * ROWS
    saved = [shape(total, 128)] + [shape(total, D)] * 4 + [shape(total, HEADS * ROWS)] + [shape(total, D)] * 2
    rooms = [pltpu.VMEM(a.shape, jnp.float32) for a in saved]
    la, h2, *kept = local(
        forward_kernel, [shape(count, 128), shape(count, D)], at, (walk, nuc, b_mlp, wout), 61,
        (w_embed,) + mats, saved,
        [pltpu.VMEM((FEAT, D), jnp.float32), pltpu.VMEM((5, D, D), jnp.float32)]
        + rooms
        + [pltpu.SemaphoreType.DMA((6,)), pltpu.SemaphoreType.DMA((14,))],
    )

    logs = everyone(la[:, 0], ("ylo", "core", "x", "yh", "z"), groups * nx * ny * nz)
    logs = logs.reshape(groups, nx, ny, nz, states, ny)
    every = logs.transpose(0, 2, 4, 1, 5, 3).reshape(states, states, walker_count)
    home = jnp.diagonal(every, axis1=0, axis2=1).T
    margins = jnp.mean(jnp.exp(every - home[None]), axis=2).T
    zi = lax.axis_index("z")
    logs = lax.dynamic_index_in_dim(lax.dynamic_index_in_dim(logs, xi, 1, False), zi, 2, False)
    logs = logs.reshape(states, states, ny)
    home = jnp.diagonal(logs, axis1=0, axis2=1).T
    ratios = jnp.exp(logs - home[None])
    identity = jnp.eye(states, dtype=jnp.float32)
    coupling = margins.T * (1.0 - identity)
    denominator = jnp.sum(coupling[:, :, None] * ratios.transpose(1, 0, 2), axis=1) / walker_count
    cot = coupling.T[:, :, None] * ratios / walker_count - identity[:, :, None] * denominator[None]
    own = lax.dynamic_index_in_dim(cot, net, 0, False).reshape(count)
    own = jnp.broadcast_to(own[:, None], (count, 128))

    place = jnp.stack([xi, yh]).astype(jnp.int32)
    pieces = local(
        backward_kernel, [shape(BLOCK, D)] * 4, place, (own, h2, b_mlp, wout), 61,
        tuple(kept) + mats, (),
        [pltpu.VMEM((5, D, D), jnp.float32)]
        + rooms
        + [pltpu.VMEM((total, D), jnp.float32), pltpu.VMEM((total, 3 * D), jnp.float32),
           pltpu.VMEM((SPLIT, BLOCK, D), jnp.float32), pltpu.SemaphoreType.DMA((32,))],
    )
    mine = pieces[0]
    for d, piece in zip((2, 1, -1), pieces[1:]):
        mine = mine + shift(piece, "x", d, nx)
    mine = jnp.sum(
        lax.all_to_all(mine.reshape(nz, BLOCK // nz, D), "z", 0, 0, tiled=False), axis=0
    )
    mine = everyone(mine, "z", nz).reshape(BLOCK, D)
    a, c = mine[:HALF], mine[HALF:]
    a_far = shift(a, "yh", 1, ny)
    c_far = [shift(c, "x", d, nx) for d in (2, 1, -1)]
    a_far, *c_far = lax.optimization_barrier((a_far, *c_far))
    a = jnp.stack([a, a_far])
    c = jnp.stack([c, *c_far])
    arrays = [a] + [shift(a, "x", d, nx) for d in (2, 1, -1)] + [c, shift(c, "yh", 1, ny)]
    mat = shape(2, D, D)
    mlp, attn, query, key, value, embed, bias, out = local(
        assemble_kernel, [mat] * 5 + [shape(2, FEAT, D), shape(2, 1, D), shape(2, 1, D)],
        place, arrays, 4,
    )
    return (
        margins, embed, query[:, None], key[:, None], value[:, None],
        attn[:, None], mlp[:, None], bias, out[:, 0],
    )


def solution(mesh):
    fine = Mesh(mesh.devices.reshape(2, 2, 4, 2, 8), ("ylo", "core", "x", "yh", "z"))
    s, w = ("ylo", "core"), ("x", "yh", "z")
    return jax.shard_map(
        shards,
        mesh=fine,
        in_specs=(P(s, w, None), P()) + (P(s),) * 8,
        out_specs=(P(),) + (P(s),) * 8,
        check_vma=False,
    )
```

```python
import jax
import jax.numpy as jnp
from jax import lax
from jax.experimental import pallas as pl
from jax.experimental.pallas import tpu as pltpu
from jax.sharding import Mesh, PartitionSpec as P

HEADS = 4
NE = 42
ROWS = 48
D = 256
FEAT = 48
EPS = 1e-05
HIGHEST = lax.Precision.HIGHEST
NN = (((1,), (0,)), ((), ()))
NT = (((1,), (1,)), ((), ()))
TN = (((0,), (0,)), ((), ()))
UNROLL = 4


def exact(a, b, dims):
    return lax.dot_general(a, b, dims, precision=HIGHEST, preferred_element_type=jnp.float32)


def halves(a):
    high = a.astype(jnp.bfloat16)
    return high, (a - high.astype(jnp.float32)).astype(jnp.bfloat16)


def three(a, b, dims):
    def one(x, y):
        return lax.dot_general(x, y, dims, preferred_element_type=jnp.float32)

    return one(a[0], b[0]) + (one(a[0], b[1]) + one(a[1], b[0]))


def stacked_tn(a, b):
    left = jnp.concatenate([a[0], a[0], a[1]], axis=0)
    right = jnp.concatenate([b[0], b[1], b[0]], axis=0)
    return lax.dot_general(left, right, TN, preferred_element_type=jnp.float32)


def normalise(hidden):
    centre = hidden - jnp.mean(hidden, axis=-1, keepdims=True)
    scale = lax.rsqrt(jnp.mean(centre * centre, axis=-1, keepdims=True) + EPS)
    return centre * scale, scale


def normalise_back(grad, normed, scale):
    return scale * (
        grad
        - jnp.mean(grad, axis=-1, keepdims=True)
        - normed * jnp.mean(grad * normed, axis=-1, keepdims=True)
    )


def head_masks():
    lane = lax.broadcasted_iota(jnp.int32, (1, D), 1)
    return [(lane // (D // HEADS)) == h for h in range(HEADS)]


def spread(block, masks):
    return jnp.concatenate([jnp.where(m, block, 0.0) for m in masks], axis=0)


def gather_heads(stacked, masks):
    out = jnp.where(masks[0], stacked[:ROWS], 0.0)
    for h in range(1, HEADS):
        out = out + jnp.where(masks[h], stacked[h * ROWS : (h + 1) * ROWS], 0.0)
    return out


def fetch(source, target, sem):
    copy = pltpu.make_async_copy(source, target, sem)
    copy.start()
    return copy


def piece(source, target, step, sem):
    size = UNROLL * ROWS
    rows = pl.ds(step * size, size)
    if not isinstance(step, int):
        rows = pl.ds(pl.multiple_of(step * size, size), size)
    return pltpu.make_async_copy(source.at[rows], target.at[rows], sem)


def forward_kernel(
    net_ref, walk_ref, nuc_ref, b_ref, wout_ref, we_hbm, wq_hbm, wk_hbm, wv_hbm, wo_hbm, wm_hbm,
    la_ref, h2_ref, feat_hbm, x_hbm, q_hbm, k_hbm, v_hbm, at_hbm, mix_hbm, h1_hbm,
    we_ref, w_ref, feat_ref, x_ref, q_ref, k_ref, v_ref, at_ref, mix_ref, h1_ref, in_sem, out_sem,
):
    at = net_ref[0]
    loads = [fetch(we_hbm.at[at], we_ref, in_sem.at[0])]
    for i, w in enumerate((wq_hbm, wk_hbm, wv_hbm, wo_hbm, wm_hbm)):
        loads.append(fetch(w.at[at, 0], w_ref.at[i], in_sem.at[1 + i]))
    count = walk_ref.shape[0]
    width = walk_ref.shape[1]
    electron = lax.broadcasted_iota(jnp.int32, (ROWS, width), 0)
    lane = lax.broadcasted_iota(jnp.int32, (ROWS, width), 1)
    picks = [lane == 3 * electron + c for c in range(3)]
    flane = lax.broadcasted_iota(jnp.int32, (1, FEAT), 1)
    kind = flane % 4
    masks = head_masks()
    n = [nuc_ref[c : c + 1, :] for c in range(3)]
    for w in range(count):
        row = jnp.broadcast_to(walk_ref[w : w + 1, :], (ROWS, width))
        off = [
            jnp.sum(jnp.where(picks[c], row, 0.0), axis=1, keepdims=True) - n[c] for c in range(3)
        ]
        dist = jnp.sqrt(off[0] * off[0] + off[1] * off[1] + off[2] * off[2] + 1.0)
        feat = jnp.where(kind == 0, off[0], jnp.where(kind == 1, off[1], jnp.where(kind == 2, off[2], dist)))
        feat_ref[w * ROWS : (w + 1) * ROWS, :FEAT] = feat
    loads[0].wait()
    h0 = exact(feat_ref[:, :FEAT], we_ref[...], NN)
    x, r1 = normalise(h0)
    feat_ref[:, FEAT : FEAT + 1] = r1
    x_ref[...] = x
    stores = [fetch(x_ref, x_hbm, out_sem.at[0]), fetch(feat_ref, feat_hbm, out_sem.at[4])]
    loads[1].wait()
    q_ref[...] = exact(x, w_ref[0], NN) * 0.125
    stores.append(fetch(q_ref, q_hbm, out_sem.at[1]))
    loads[2].wait()
    k_ref[...] = exact(x, w_ref[1], NN)
    stores.append(fetch(k_ref, k_hbm, out_sem.at[2]))
    loads[3].wait()
    v_ref[...] = three(halves(x), halves(w_ref[2]), NN)
    stores.append(fetch(v_ref, v_hbm, out_sem.at[3]))
    key_row = lax.broadcasted_iota(jnp.int32, (ROWS, HEADS * ROWS), 0)

    def attend(step, carry):
        spans = [
            pl.ds(pl.multiple_of(step * (UNROLL * ROWS) + u * ROWS, ROWS), ROWS) for u in range(UNROLL)
        ]
        scores = [exact(k_ref[rows, :], spread(q_ref[rows, :], masks), NT) for rows in spans]
        scores = [jnp.where(key_row < NE, a, -1e30) for a in scores]
        weights = [jnp.exp(a - jnp.max(a, axis=0, keepdims=True)) for a in scores]
        attention = [a / jnp.sum(a, axis=0, keepdims=True) for a in weights]
        for rows, a in zip(spans, attention):
            at_ref[rows, :] = a
        mixed = [stacked_tn(halves(a), halves(v_ref[rows, :])) for rows, a in zip(spans, attention)]
        for rows, a in zip(spans, mixed):
            mix_ref[rows, :] = gather_heads(a, masks)
        for i, (a, b) in enumerate(((at_ref, at_hbm), (mix_ref, mix_hbm))):
            piece(a, b, step, out_sem.at[6 + 4 * i + step]).start()
        return carry

    lax.fori_loop(0, count // UNROLL, attend, 0)
    for step in range(count // UNROLL):
        for i, (a, b) in enumerate(((at_ref, at_hbm), (mix_ref, mix_hbm))):
            stores.append(piece(a, b, step, out_sem.at[6 + 4 * i + step]))
    loads[4].wait()
    h1 = h0 + three(halves(mix_ref[...]), halves(w_ref[3]), NN)
    h1_ref[...] = h1
    stores.append(fetch(h1_ref, h1_hbm, out_sem.at[5]))
    y, _ = normalise(h1)
    loads[5].wait()
    t = jnp.tanh(three(halves(y), halves(w_ref[4]), NN) + b_ref[at])
    h2 = h1 + t
    real = lax.broadcasted_iota(jnp.int32, (ROWS, 1), 0) < NE
    for w in range(count):
        total = jnp.sum(jnp.where(real, h2[w * ROWS : (w + 1) * ROWS, :], 0.0), axis=0, keepdims=True) / NE
        h2_ref[w : w + 1, :] = total
        la_ref[w : w + 1, :] = jnp.broadcast_to(
            jnp.sum(total * wout_ref[at], axis=1, keepdims=True), (1, 128)
        )
    for copy in stores:
        copy.wait()


def backward_kernel(
    net_ref, b_ref, wout_ref,
    feat_hbm, x_hbm, q_hbm, k_hbm, v_hbm, at_hbm, h1_hbm,
    wq_hbm, wk_hbm, wv_hbm, wo_hbm, wm_hbm,
    y_hbm, dm_hbm, dh1_hbm, dqkv_hbm, dh0_hbm,
    w_ref, feat_ref, x_ref, q_ref, k_ref, v_ref, at_ref, h1_ref,
    do_ref, dqkv_ref, y_ref, dm_ref, dh1_ref, dh0_ref, sem, out_sem,
):
    at = net_ref[0]
    count = x_ref.shape[0] // ROWS
    steps = count // UNROLL
    first = [
        fetch(h1_hbm, h1_ref, sem.at[0]),
        fetch(wm_hbm.at[at, 0], w_ref.at[4], sem.at[1]),
        fetch(wo_hbm.at[at, 0], w_ref.at[3], sem.at[2]),
    ]
    chunked = ((at_hbm, at_ref), (v_hbm, v_ref), (q_hbm, q_ref), (k_hbm, k_ref))
    for step in range(steps):
        for i, (a, b) in enumerate(chunked):
            piece(a, b, step, sem.at[16 + steps * i + step]).start()
    later = (
        (wq_hbm.at[at, 0], w_ref.at[0]), (wk_hbm.at[at, 0], w_ref.at[1]), (wv_hbm.at[at, 0], w_ref.at[2]),
        (x_hbm, x_ref), (feat_hbm, feat_ref),
    )
    later = [fetch(a, b, sem.at[3 + i]) for i, (a, b) in enumerate(later)]
    masks = head_masks()
    row = lax.broadcasted_iota(jnp.int32, (count * ROWS, 1), 0)
    g = jnp.where(row % ROWS < NE, wout_ref[at] / NE, 0.0)
    first[0].wait()
    y, r2 = normalise(h1_ref[...])
    y_ref[...] = y
    stores = [fetch(y_ref, y_hbm, out_sem.at[0])]
    y_parts = halves(y)
    first[1].wait()
    wm = halves(w_ref[4])
    t = jnp.tanh(three(y_parts, wm, NN) + b_ref[at])
    dm = g * (1.0 - t * t)
    dm_ref[...] = dm
    stores.append(fetch(dm_ref, dm_hbm, out_sem.at[1]))
    dy = three(halves(dm), wm, NT)
    dh1 = g + normalise_back(dy, y, r2)
    dh1_ref[...] = dh1
    stores.append(fetch(dh1_ref, dh1_hbm, out_sem.at[2]))
    first[2].wait()
    do_ref[...] = three(halves(dh1), halves(w_ref[3]), NT)

    def attend(step, carry):
        for i, (a, b) in enumerate(chunked):
            piece(a, b, step, sem.at[16 + steps * i + step]).wait()
        spans = [
            pl.ds(pl.multiple_of(step * (UNROLL * ROWS) + u * ROWS, ROWS), ROWS) for u in range(UNROLL)
        ]
        attention = [at_ref[rows, :] for rows in spans]
        do = [halves(spread(do_ref[rows, :], masks)) for rows in spans]
        da = [three(halves(v_ref[rows, :]), a, NT) for rows, a in zip(spans, do)]
        dv = [three(halves(a), b, NN) for a, b in zip(attention, do)]
        ds = [a * (b - jnp.sum(b * a, axis=0, keepdims=True)) for a, b in zip(attention, da)]
        ds = [halves(a) for a in ds]
        dk = [three(a, halves(spread(q_ref[rows, :], masks)), NN) for rows, a in zip(spans, ds)]
        dq = [stacked_tn(a, halves(k_ref[rows, :])) for rows, a in zip(spans, ds)]
        for rows, a, b, c in zip(spans, dq, dk, dv):
            dqkv_ref[rows, :D] = gather_heads(a, masks) * 0.125
            dqkv_ref[rows, D : 2 * D] = b
            dqkv_ref[rows, 2 * D :] = c
        piece(dqkv_ref, dqkv_hbm, step, out_sem.at[4 + step]).start()
        return carry

    lax.fori_loop(0, steps, attend, 0)
    for step in range(steps):
        stores.append(piece(dqkv_ref, dqkv_hbm, step, out_sem.at[4 + step]))
    for copy in later:
        copy.wait()
    dx = None
    for i in range(3):
        term = three(halves(dqkv_ref[:, i * D : (i + 1) * D]), halves(w_ref[i]), NT)
        dx = term if dx is None else dx + term
    dh0_ref[...] = dh1 + normalise_back(dx, x_ref[...], feat_ref[:, FEAT : FEAT + 1])
    stores.append(fetch(dh0_ref, dh0_hbm, out_sem.at[3]))
    for copy in stores:
        copy.wait()


def weights_kernel(
    where_ref, c_ref, h2_ref,
    feat_hbm, x_hbm, mix_hbm, y_hbm, dm_hbm, dh1_hbm, dqkv_hbm, dh0_hbm,
    own_ref, far_ref, up_ref, down_ref,
    feat_ref, x_ref, mix_ref, y_ref, dm_ref, dh1_ref, dqkv_ref, dh0_ref, out_ref, sem,
):
    order = (
        (y_hbm, y_ref), (dm_hbm, dm_ref), (mix_hbm, mix_ref), (dh1_hbm, dh1_ref), (x_hbm, x_ref),
        (dqkv_hbm, dqkv_ref), (feat_hbm, feat_ref), (dh0_hbm, dh0_ref),
    )
    loads = [fetch(a, b, sem.at[i]) for i, (a, b) in enumerate(order)]
    me = where_ref[0]
    count = c_ref.shape[0]
    factor = jnp.concatenate(
        [jnp.broadcast_to(c_ref[w : w + 1, :1], (ROWS, 1)) for w in range(count)], axis=0
    )

    def put(i, value):
        for block in range(SPLIT):
            out_ref[block, i * PART : (i + 1) * PART, :] = value[block * PART : (block + 1) * PART, :]

    loads[0].wait()
    loads[1].wait()
    dm = factor * dm_ref[...]
    put(0, three(halves(y_ref[...]), halves(dm), TN))
    loads[2].wait()
    loads[3].wait()
    put(1, three(halves(mix_ref[...]), halves(factor * dh1_ref[...]), TN))
    loads[4].wait()
    loads[5].wait()
    x = halves(x_ref[...])
    for i in range(3):
        put(2 + i, three(x, halves(factor * dqkv_ref[:, i * D : (i + 1) * D]), TN))
    loads[6].wait()
    loads[7].wait()
    base = 5 * PART
    embed = three(halves(feat_ref[:, :FEAT]), halves(factor * dh0_ref[...]), TN)
    for block in range(SPLIT - 1):
        out_ref[block, base:, :] = embed[block * TAIL : (block + 1) * TAIL, :]
    out_ref[SPLIT - 1, base:, :] = jnp.concatenate(
        [
            jnp.sum(dm, axis=0, keepdims=True),
            jnp.sum(c_ref[:, :1] * h2_ref[...], axis=0, keepdims=True),
            jnp.zeros((TAIL - 2, D), jnp.float32),
        ],
        axis=0,
    )
    for ref, d in ((own_ref, 0), (far_ref, 2), (up_ref, 1), (down_ref, 3)):
        ref[...] = out_ref[(me + d) % SPLIT]


def assemble_kernel(
    where_ref, a0_ref, a1_ref, a2_ref, a3_ref, c0_ref, c1_ref,
    mlp_ref, attn_ref, query_ref, key_ref, value_ref, embed_ref, bias_ref, out_ref,
):
    me, yh = where_ref[0], where_ref[1]
    mats = (mlp_ref, attn_ref, query_ref, key_ref, value_ref)
    for slot, (d, a_ref) in enumerate(((0, a0_ref), (2, a1_ref), (1, a2_ref), (3, a3_ref))):
        block = (me + SPLIT - d) % SPLIT
        start = pl.multiple_of(block * PART, PART)
        for pair, c_ref in enumerate((c0_ref, c1_ref)):
            net = yh if pair == 0 else 1 - yh
            for i in range(5):
                low, high = i * PART, (i + 1) * PART
                cut = min(max(low, HALF), high)
                if cut > low:
                    mats[i][net, pl.ds(start, cut - low), :] = a_ref[pair, low:cut, :]
                if high > cut:
                    mats[i][net, pl.ds(pl.multiple_of(start + (cut - low), 8), high - cut), :] = c_ref[
                        slot, cut - HALF : high - HALF, :
                    ]
            base = 5 * PART - HALF

            @pl.when(block < SPLIT - 1)
            def _():
                embed_ref[net, pl.ds(pl.multiple_of(block * TAIL, TAIL), TAIL), :] = c_ref[slot, base:, :]

            @pl.when(block == SPLIT - 1)
            def _():
                bias_ref[net] = c_ref[slot, base : base + 1, :]
                out_ref[net] = c_ref[slot, base + 1 : base + 2, :]


SPLIT = 4
PART = 64
TAIL = 16
HALF = 168
BLOCK = 336


def vmem():
    return pl.BlockSpec(memory_space=pltpu.VMEM)


def shape(*s):
    return jax.ShapeDtypeStruct(s, jnp.float32)


def local(kernel, outs, at, plain, limit, far=(), far_outs=(), scratch=()):
    anywhere = pl.BlockSpec(memory_space=pltpu.MemorySpace.HBM)
    return pl.pallas_call(
        kernel,
        out_shape=list(outs) + list(far_outs),
        in_specs=[pl.BlockSpec(memory_space=pltpu.SMEM)] + [vmem() for _ in plain] + [anywhere for _ in far],
        out_specs=[vmem() for _ in outs] + [anywhere for _ in far_outs],
        scratch_shapes=list(scratch),
        compiler_params=pltpu.CompilerParams(vmem_limit_bytes=limit * 1024 * 1024),
    )(at, *plain, *far)


def offsets(n):
    return [n // 2] + [d for k in range(1, n // 2) for d in (k, -k)] if n > 2 else [1]


def shift(v, axis, d, n):
    return lax.ppermute(v, axis, [(i, (i + d) % n) for i in range(n)])


def gather(v, axis, n):
    me = lax.axis_index(axis)
    out = jnp.zeros((n,) + v.shape, v.dtype)
    out = lax.dynamic_update_index_in_dim(out, v, me, 0)
    for d in offsets(n):
        out = lax.dynamic_update_index_in_dim(out, shift(v, axis, d, n), (me - d) % n, 0)
    return out


def scatter_sum(v, axis, n):
    me = lax.axis_index(axis)
    blocks = v.reshape((n, v.shape[0] // n) + v.shape[1:])
    total = lax.dynamic_index_in_dim(blocks, me, 0, False)
    for d in offsets(n):
        total = total + shift(lax.dynamic_index_in_dim(blocks, (me + d) % n, 0, False), axis, d, n)
    return total


def everyone(v, axes, n):
    return lax.all_to_all(jnp.broadcast_to(v[None], (n,) + v.shape), axes, 0, 0, tiled=False)


def shards(walkers, nuclei, w_embed, w_query, w_key, w_value, w_attn_out, w_mlp, b_mlp, w_out):
    nx, ny, nz = lax.axis_size("x"), lax.axis_size("yh"), lax.axis_size("z")
    groups = lax.axis_size("ylo") * lax.axis_size("core")
    walker_count = nx * ny * nz
    xi, yh = lax.axis_index("x"), lax.axis_index("yh")
    state = lax.axis_index("ylo") * lax.axis_size("core") + lax.axis_index("core")
    states = 2 * groups
    net = state * 2 + yh
    near = ("ylo", "core", "yh")
    gathered = everyone(walkers.reshape(2, 126), near, groups * ny)
    walk = gathered.reshape(groups, ny, 2, 126).transpose(0, 2, 1, 3).reshape(states * ny, 126)
    nuc = jnp.repeat(nuclei.T, 4, axis=1)
    at = yh.reshape(1).astype(jnp.int32)
    mats = (w_query, w_key, w_value, w_attn_out, w_mlp)
    wout = w_out[:, None, :]
    count = states * ny
    total = count * ROWS
    saved = [shape(total, 128)] + [shape(total, D)] * 4 + [shape(total, HEADS * ROWS)] + [shape(total, D)] * 2
    rooms = [pltpu.VMEM(a.shape, jnp.float32) for a in saved]
    la, h2, *kept = local(
        forward_kernel, [shape(count, 128), shape(count, D)], at, (walk, nuc, b_mlp, wout), 61,
        (w_embed,) + mats, saved,
        [pltpu.VMEM((FEAT, D), jnp.float32), pltpu.VMEM((5, D, D), jnp.float32)]
        + rooms
        + [pltpu.SemaphoreType.DMA((6,)), pltpu.SemaphoreType.DMA((14,))],
    )

    feat, x, q, k, v, attn_saved, mix, h1 = kept
    grads = [shape(total, D)] * 3 + [shape(total, 3 * D), shape(total, D)]
    y, dm, dh1, dqkv, dh0 = local(
        backward_kernel, [], at, (b_mlp, wout), 61, (feat, x, q, k, v, attn_saved, h1) + mats, grads,
        [pltpu.VMEM((5, D, D), jnp.float32)]
        + rooms[:6] + rooms[7:]
        + [pltpu.VMEM((total, D), jnp.float32), pltpu.VMEM((total, 3 * D), jnp.float32)]
        + [pltpu.VMEM((total, D), jnp.float32)] * 4
        + [pltpu.SemaphoreType.DMA((32,)), pltpu.SemaphoreType.DMA((8,))],
    )

    logs = everyone(la[:, 0], near, groups * ny).reshape(states, states, ny)
    home = jnp.diagonal(logs, axis1=0, axis2=1).T
    ratios = jnp.exp(logs - home[None])
    part = jnp.sum(ratios, axis=2).T
    sums = jnp.sum(everyone(part, ("x", "z"), nx * nz), axis=0)
    margins = sums / walker_count
    identity = jnp.eye(states, dtype=jnp.float32)
    coupling = margins.T * (1.0 - identity)
    denominator = jnp.sum(coupling[:, :, None] * ratios.transpose(1, 0, 2), axis=1) / walker_count
    cot = coupling.T[:, :, None] * ratios / walker_count - identity[:, :, None] * denominator[None]
    own = lax.dynamic_index_in_dim(cot, net, 0, False).reshape(count)
    own = jnp.broadcast_to(own[:, None], (count, 128))

    place = jnp.stack([xi, yh]).astype(jnp.int32)
    sources = (feat, x, mix, y, dm, dh1, dqkv, dh0)
    pieces = local(
        weights_kernel, [shape(BLOCK, D)] * 4, place, (own, h2), 61, sources, (),
        [pltpu.VMEM(a.shape, jnp.float32) for a in sources]
        + [pltpu.VMEM((SPLIT, BLOCK, D), jnp.float32), pltpu.SemaphoreType.DMA((8,))],
    )
    mine = pieces[0]
    for d, piece in zip((2, 1, -1), pieces[1:]):
        mine = mine + shift(piece, "x", d, nx)
    mine = jnp.sum(
        lax.all_to_all(mine.reshape(nz, BLOCK // nz, D), "z", 0, 0, tiled=False), axis=0
    )
    mine = everyone(mine, "z", nz).reshape(BLOCK, D)
    a, c = mine[:HALF], mine[HALF:]
    a_far = shift(a, "yh", 1, ny)
    c_far = [shift(c, "x", d, nx) for d in (2, 1, -1)]
    a_far, *c_far = lax.optimization_barrier((a_far, *c_far))
    a = jnp.stack([a, a_far])
    c = jnp.stack([c, *c_far])
    arrays = [a] + [shift(a, "x", d, nx) for d in (2, 1, -1)] + [c, shift(c, "yh", 1, ny)]
    mat = shape(2, D, D)
    mlp, attn, query, key, value, embed, bias, out = local(
        assemble_kernel, [mat] * 5 + [shape(2, FEAT, D), shape(2, 1, D), shape(2, 1, D)],
        place, arrays, 4,
    )
    return (
        margins, embed, query[:, None], key[:, None], value[:, None],
        attn[:, None], mlp[:, None], bias, out[:, 0],
    )


def solution(mesh):
    fine = Mesh(mesh.devices.reshape(2, 2, 4, 2, 8), ("ylo", "core", "x", "yh", "z"))
    s, w = ("ylo", "core"), ("x", "yh", "z")
    return jax.shard_map(
        shards,
        mesh=fine,
        in_specs=(P(s, w, None), P()) + (P(s),) * 8,
        out_specs=(P(),) + (P(s),) * 8,
        check_vma=False,
    )
```

```python
import jax
import jax.numpy as jnp
from jax import lax
from jax.experimental import pallas as pl
from jax.experimental.pallas import tpu as pltpu
from jax.sharding import Mesh, PartitionSpec as P

HEADS = 4
NE = 42
ROWS = 48
D = 256
FEAT = 48
EPS = 1e-05
HIGHEST = lax.Precision.HIGHEST
NN = (((1,), (0,)), ((), ()))
NT = (((1,), (1,)), ((), ()))
TN = (((0,), (0,)), ((), ()))
UNROLL = 4


def exact(a, b, dims):
    return lax.dot_general(a, b, dims, precision=HIGHEST, preferred_element_type=jnp.float32)


def halves(a):
    high = a.astype(jnp.bfloat16)
    return high, (a - high.astype(jnp.float32)).astype(jnp.bfloat16)


def three(a, b, dims):
    def one(x, y):
        return lax.dot_general(x, y, dims, preferred_element_type=jnp.float32)

    return one(a[0], b[0]) + (one(a[0], b[1]) + one(a[1], b[0]))


def stacked_tn(a, b):
    left = jnp.concatenate([a[0], a[0], a[1]], axis=0)
    right = jnp.concatenate([b[0], b[1], b[0]], axis=0)
    return lax.dot_general(left, right, TN, preferred_element_type=jnp.float32)


def normalise(hidden):
    centre = hidden - jnp.mean(hidden, axis=-1, keepdims=True)
    scale = lax.rsqrt(jnp.mean(centre * centre, axis=-1, keepdims=True) + EPS)
    return centre * scale, scale


def normalise_back(grad, normed, scale):
    return scale * (
        grad
        - jnp.mean(grad, axis=-1, keepdims=True)
        - normed * jnp.mean(grad * normed, axis=-1, keepdims=True)
    )


def head_masks():
    lane = lax.broadcasted_iota(jnp.int32, (1, D), 1)
    return [(lane // (D // HEADS)) == h for h in range(HEADS)]


def spread(block, masks):
    return jnp.concatenate([jnp.where(m, block, 0.0) for m in masks], axis=0)


def gather_heads(stacked, masks):
    out = jnp.where(masks[0], stacked[:ROWS], 0.0)
    for h in range(1, HEADS):
        out = out + jnp.where(masks[h], stacked[h * ROWS : (h + 1) * ROWS], 0.0)
    return out


def fetch(source, target, sem):
    copy = pltpu.make_async_copy(source, target, sem)
    copy.start()
    return copy


def piece(source, target, step, sem):
    size = UNROLL * ROWS
    rows = pl.ds(step * size, size)
    if not isinstance(step, int):
        rows = pl.ds(pl.multiple_of(step * size, size), size)
    return pltpu.make_async_copy(source.at[rows], target.at[rows], sem)


def forward_kernel(
    net_ref, walk_ref, nuc_ref, b_ref, wout_ref, we_hbm, wq_hbm, wk_hbm, wv_hbm, wo_hbm, wm_hbm,
    la_ref, h2_ref, feat_hbm, x_hbm, q_hbm, k_hbm, v_hbm, at_hbm, mix_hbm, h1_hbm,
    we_ref, w_ref, feat_ref, x_ref, q_ref, k_ref, v_ref, at_ref, mix_ref, h1_ref, in_sem, out_sem,
):
    at = net_ref[0]
    loads = [fetch(we_hbm.at[at], we_ref, in_sem.at[0])]
    for i, w in enumerate((wq_hbm, wk_hbm, wv_hbm, wo_hbm, wm_hbm)):
        loads.append(fetch(w.at[at, 0], w_ref.at[i], in_sem.at[1 + i]))
    count = walk_ref.shape[0]
    width = walk_ref.shape[1]
    electron = lax.broadcasted_iota(jnp.int32, (ROWS, width), 0)
    lane = lax.broadcasted_iota(jnp.int32, (ROWS, width), 1)
    picks = [lane == 3 * electron + c for c in range(3)]
    flane = lax.broadcasted_iota(jnp.int32, (1, FEAT), 1)
    kind = flane % 4
    masks = head_masks()
    n = [nuc_ref[c : c + 1, :] for c in range(3)]
    for w in range(count):
        row = jnp.broadcast_to(walk_ref[w : w + 1, :], (ROWS, width))
        off = [
            jnp.sum(jnp.where(picks[c], row, 0.0), axis=1, keepdims=True) - n[c] for c in range(3)
        ]
        dist = jnp.sqrt(off[0] * off[0] + off[1] * off[1] + off[2] * off[2] + 1.0)
        feat = jnp.where(kind == 0, off[0], jnp.where(kind == 1, off[1], jnp.where(kind == 2, off[2], dist)))
        feat_ref[w * ROWS : (w + 1) * ROWS, :FEAT] = feat
    loads[0].wait()
    h0 = exact(feat_ref[:, :FEAT], we_ref[...], NN)
    x, r1 = normalise(h0)
    feat_ref[:, FEAT : FEAT + 1] = r1
    x_ref[...] = x
    stores = [fetch(x_ref, x_hbm, out_sem.at[0]), fetch(feat_ref, feat_hbm, out_sem.at[4])]
    loads[1].wait()
    q_ref[...] = exact(x, w_ref[0], NN) * 0.125
    stores.append(fetch(q_ref, q_hbm, out_sem.at[1]))
    loads[2].wait()
    k_ref[...] = exact(x, w_ref[1], NN)
    stores.append(fetch(k_ref, k_hbm, out_sem.at[2]))
    loads[3].wait()
    v_ref[...] = three(halves(x), halves(w_ref[2]), NN)
    stores.append(fetch(v_ref, v_hbm, out_sem.at[3]))
    key_row = lax.broadcasted_iota(jnp.int32, (ROWS, HEADS * ROWS), 0)

    def attend(step, carry):
        spans = [
            pl.ds(pl.multiple_of(step * (UNROLL * ROWS) + u * ROWS, ROWS), ROWS) for u in range(UNROLL)
        ]
        scores = [exact(k_ref[rows, :], spread(q_ref[rows, :], masks), NT) for rows in spans]
        scores = [jnp.where(key_row < NE, a, -1e30) for a in scores]
        weights = [jnp.exp(a - jnp.max(a, axis=0, keepdims=True)) for a in scores]
        attention = [a / jnp.sum(a, axis=0, keepdims=True) for a in weights]
        for rows, a in zip(spans, attention):
            at_ref[rows, :] = a
        mixed = [stacked_tn(halves(a), halves(v_ref[rows, :])) for rows, a in zip(spans, attention)]
        for rows, a in zip(spans, mixed):
            mix_ref[rows, :] = gather_heads(a, masks)
        for i, (a, b) in enumerate(((at_ref, at_hbm), (mix_ref, mix_hbm))):
            piece(a, b, step, out_sem.at[6 + 4 * i + step]).start()
        return carry

    lax.fori_loop(0, count // UNROLL, attend, 0)
    for step in range(count // UNROLL):
        for i, (a, b) in enumerate(((at_ref, at_hbm), (mix_ref, mix_hbm))):
            stores.append(piece(a, b, step, out_sem.at[6 + 4 * i + step]))
    loads[4].wait()
    h1 = h0 + three(halves(mix_ref[...]), halves(w_ref[3]), NN)
    h1_ref[...] = h1
    stores.append(fetch(h1_ref, h1_hbm, out_sem.at[5]))
    y, _ = normalise(h1)
    loads[5].wait()
    t = jnp.tanh(three(halves(y), halves(w_ref[4]), NN) + b_ref[at])
    h2 = h1 + t
    real = lax.broadcasted_iota(jnp.int32, (ROWS, 1), 0) < NE
    for w in range(count):
        total = jnp.sum(jnp.where(real, h2[w * ROWS : (w + 1) * ROWS, :], 0.0), axis=0, keepdims=True) / NE
        h2_ref[w : w + 1, :] = total
        la_ref[w : w + 1, :] = jnp.broadcast_to(
            jnp.sum(total * wout_ref[at], axis=1, keepdims=True), (1, 128)
        )
    for copy in stores:
        copy.wait()


def backward_kernel(
    net_ref, b_ref, wout_ref,
    feat_hbm, x_hbm, q_hbm, k_hbm, v_hbm, at_hbm, h1_hbm,
    wq_hbm, wk_hbm, wv_hbm, wo_hbm, wm_hbm,
    y_hbm, dm_hbm, dh1_hbm, dqkv_hbm, dh0_hbm,
    w_ref, feat_ref, x_ref, q_ref, k_ref, v_ref, at_ref, h1_ref,
    do_ref, dqkv_ref, y_ref, dm_ref, dh1_ref, dh0_ref, sem, out_sem,
):
    at = net_ref[0]
    count = x_ref.shape[0] // ROWS
    steps = count // UNROLL
    first = [
        fetch(h1_hbm, h1_ref, sem.at[0]),
        fetch(wm_hbm.at[at, 0], w_ref.at[4], sem.at[1]),
        fetch(wo_hbm.at[at, 0], w_ref.at[3], sem.at[2]),
    ]
    chunked = ((at_hbm, at_ref), (v_hbm, v_ref), (q_hbm, q_ref), (k_hbm, k_ref))
    for step in range(steps):
        for i, (a, b) in enumerate(chunked):
            piece(a, b, step, sem.at[16 + steps * i + step]).start()
    later = (
        (wq_hbm.at[at, 0], w_ref.at[0]), (wk_hbm.at[at, 0], w_ref.at[1]), (wv_hbm.at[at, 0], w_ref.at[2]),
        (x_hbm, x_ref), (feat_hbm, feat_ref),
    )
    later = [fetch(a, b, sem.at[3 + i]) for i, (a, b) in enumerate(later)]
    masks = head_masks()
    row = lax.broadcasted_iota(jnp.int32, (count * ROWS, 1), 0)
    g = jnp.where(row % ROWS < NE, wout_ref[at] / NE, 0.0)
    first[0].wait()
    y, r2 = normalise(h1_ref[...])
    y_ref[...] = y
    stores = [fetch(y_ref, y_hbm, out_sem.at[0])]
    y_parts = halves(y)
    first[1].wait()
    wm = halves(w_ref[4])
    t = jnp.tanh(three(y_parts, wm, NN) + b_ref[at])
    dm = g * (1.0 - t * t)
    dm_ref[...] = dm
    stores.append(fetch(dm_ref, dm_hbm, out_sem.at[1]))
    dy = three(halves(dm), wm, NT)
    dh1 = g + normalise_back(dy, y, r2)
    dh1_ref[...] = dh1
    stores.append(fetch(dh1_ref, dh1_hbm, out_sem.at[2]))
    first[2].wait()
    do_ref[...] = three(halves(dh1), halves(w_ref[3]), NT)

    def attend(step, carry):
        for i, (a, b) in enumerate(chunked):
            piece(a, b, step, sem.at[16 + steps * i + step]).wait()
        spans = [
            pl.ds(pl.multiple_of(step * (UNROLL * ROWS) + u * ROWS, ROWS), ROWS) for u in range(UNROLL)
        ]
        attention = [at_ref[rows, :] for rows in spans]
        do = [halves(spread(do_ref[rows, :], masks)) for rows in spans]
        da = [three(halves(v_ref[rows, :]), a, NT) for rows, a in zip(spans, do)]
        dv = [three(halves(a), b, NN) for a, b in zip(attention, do)]
        ds = [a * (b - jnp.sum(b * a, axis=0, keepdims=True)) for a, b in zip(attention, da)]
        ds = [halves(a) for a in ds]
        dk = [three(a, halves(spread(q_ref[rows, :], masks)), NN) for rows, a in zip(spans, ds)]
        dq = [stacked_tn(a, halves(k_ref[rows, :])) for rows, a in zip(spans, ds)]
        for rows, a, b, c in zip(spans, dq, dk, dv):
            dqkv_ref[rows, :D] = gather_heads(a, masks) * 0.125
            dqkv_ref[rows, D : 2 * D] = b
            dqkv_ref[rows, 2 * D :] = c
        piece(dqkv_ref, dqkv_hbm, step, out_sem.at[4 + step]).start()
        return carry

    lax.fori_loop(0, steps, attend, 0)
    for step in range(steps):
        stores.append(piece(dqkv_ref, dqkv_hbm, step, out_sem.at[4 + step]))
    for copy in later:
        copy.wait()
    dx = None
    for i in range(3):
        term = three(halves(dqkv_ref[:, i * D : (i + 1) * D]), halves(w_ref[i]), NT)
        dx = term if dx is None else dx + term
    dh0_ref[...] = dh1 + normalise_back(dx, x_ref[...], feat_ref[:, FEAT : FEAT + 1])
    stores.append(fetch(dh0_ref, dh0_hbm, out_sem.at[3]))
    for copy in stores:
        copy.wait()


def weights_kernel(
    where_ref, c_ref, h2_ref,
    feat_hbm, x_hbm, mix_hbm, y_hbm, dm_hbm, dh1_hbm, dqkv_hbm, dh0_hbm,
    own_ref, far_ref, up_ref, down_ref,
    feat_ref, x_ref, mix_ref, y_ref, dm_ref, dh1_ref, dqkv_ref, dh0_ref, out_ref, sem,
):
    order = (
        (y_hbm, y_ref), (dm_hbm, dm_ref), (mix_hbm, mix_ref), (dh1_hbm, dh1_ref), (x_hbm, x_ref),
        (dqkv_hbm, dqkv_ref), (feat_hbm, feat_ref), (dh0_hbm, dh0_ref),
    )
    loads = [fetch(a, b, sem.at[i]) for i, (a, b) in enumerate(order)]
    me = where_ref[0]
    count = c_ref.shape[0]
    factor = jnp.concatenate(
        [jnp.broadcast_to(c_ref[w : w + 1, :1], (ROWS, 1)) for w in range(count)], axis=0
    )

    def put(i, value):
        for block in range(SPLIT):
            out_ref[block, i * PART : (i + 1) * PART, :] = value[block * PART : (block + 1) * PART, :]

    loads[0].wait()
    loads[1].wait()
    dm = factor * dm_ref[...]
    put(0, three(halves(y_ref[...]), halves(dm), TN))
    loads[2].wait()
    loads[3].wait()
    put(1, three(halves(mix_ref[...]), halves(factor * dh1_ref[...]), TN))
    loads[4].wait()
    loads[5].wait()
    x = halves(x_ref[...])
    for i in range(3):
        put(2 + i, three(x, halves(factor * dqkv_ref[:, i * D : (i + 1) * D]), TN))
    loads[6].wait()
    loads[7].wait()
    base = 5 * PART
    embed = three(halves(feat_ref[:, :FEAT]), halves(factor * dh0_ref[...]), TN)
    for block in range(SPLIT - 1):
        out_ref[block, base:, :] = embed[block * TAIL : (block + 1) * TAIL, :]
    out_ref[SPLIT - 1, base:, :] = jnp.concatenate(
        [
            jnp.sum(dm, axis=0, keepdims=True),
            jnp.sum(c_ref[:, :1] * h2_ref[...], axis=0, keepdims=True),
            jnp.zeros((TAIL - 2, D), jnp.float32),
        ],
        axis=0,
    )
    for ref, d in ((own_ref, 0), (far_ref, 2), (up_ref, 1), (down_ref, 3)):
        ref[...] = out_ref[(me + d) % SPLIT]


def assemble_kernel(
    where_ref, a0_ref, a1_ref, a2_ref, a3_ref, c0_ref, c1_ref,
    mlp_ref, attn_ref, query_ref, key_ref, value_ref, embed_ref, bias_ref, out_ref,
):
    me, yh = where_ref[0], where_ref[1]
    mats = (mlp_ref, attn_ref, query_ref, key_ref, value_ref)
    for slot, (d, a_ref) in enumerate(((0, a0_ref), (2, a1_ref), (1, a2_ref), (3, a3_ref))):
        block = (me + SPLIT - d) % SPLIT
        start = pl.multiple_of(block * PART, PART)
        for pair, c_ref in enumerate((c0_ref, c1_ref)):
            net = yh if pair == 0 else 1 - yh
            for i in range(5):
                low, high = i * PART, (i + 1) * PART
                cut = min(max(low, HALF), high)
                if cut > low:
                    mats[i][net, pl.ds(start, cut - low), :] = a_ref[pair, low:cut, :]
                if high > cut:
                    mats[i][net, pl.ds(pl.multiple_of(start + (cut - low), 8), high - cut), :] = c_ref[
                        slot, cut - HALF : high - HALF, :
                    ]
            base = 5 * PART - HALF

            @pl.when(block < SPLIT - 1)
            def _():
                embed_ref[net, pl.ds(pl.multiple_of(block * TAIL, TAIL), TAIL), :] = c_ref[slot, base:, :]

            @pl.when(block == SPLIT - 1)
            def _():
                bias_ref[net] = c_ref[slot, base : base + 1, :]
                out_ref[net] = c_ref[slot, base + 1 : base + 2, :]


SPLIT = 4
PART = 64
TAIL = 16
HALF = 168
BLOCK = 336


def vmem():
    return pl.BlockSpec(memory_space=pltpu.VMEM)


def shape(*s):
    return jax.ShapeDtypeStruct(s, jnp.float32)


def local(kernel, outs, at, plain, limit, far=(), far_outs=(), scratch=()):
    anywhere = pl.BlockSpec(memory_space=pltpu.MemorySpace.HBM)
    return pl.pallas_call(
        kernel,
        out_shape=list(outs) + list(far_outs),
        in_specs=[pl.BlockSpec(memory_space=pltpu.SMEM)] + [vmem() for _ in plain] + [anywhere for _ in far],
        out_specs=[vmem() for _ in outs] + [anywhere for _ in far_outs],
        scratch_shapes=list(scratch),
        compiler_params=pltpu.CompilerParams(vmem_limit_bytes=limit * 1024 * 1024),
    )(at, *plain, *far)


def offsets(n):
    return [n // 2] + [d for k in range(1, n // 2) for d in (k, -k)] if n > 2 else [1]


def shift(v, axis, d, n):
    return lax.ppermute(v, axis, [(i, (i + d) % n) for i in range(n)])


def gather(v, axis, n):
    me = lax.axis_index(axis)
    out = jnp.zeros((n,) + v.shape, v.dtype)
    out = lax.dynamic_update_index_in_dim(out, v, me, 0)
    for d in offsets(n):
        out = lax.dynamic_update_index_in_dim(out, shift(v, axis, d, n), (me - d) % n, 0)
    return out


def scatter_sum(v, axis, n):
    me = lax.axis_index(axis)
    blocks = v.reshape((n, v.shape[0] // n) + v.shape[1:])
    total = lax.dynamic_index_in_dim(blocks, me, 0, False)
    for d in offsets(n):
        total = total + shift(lax.dynamic_index_in_dim(blocks, (me + d) % n, 0, False), axis, d, n)
    return total


def everyone(v, axes, n):
    return lax.all_to_all(jnp.broadcast_to(v[None], (n,) + v.shape), axes, 0, 0, tiled=False)


def shards(walkers, nuclei, w_embed, w_query, w_key, w_value, w_attn_out, w_mlp, b_mlp, w_out):
    nx, ny, nz = lax.axis_size("x"), lax.axis_size("yh"), lax.axis_size("z")
    groups = lax.axis_size("ylo") * lax.axis_size("core")
    walker_count = nx * ny * nz
    xi, yh = lax.axis_index("x"), lax.axis_index("yh")
    state = lax.axis_index("ylo") * lax.axis_size("core") + lax.axis_index("core")
    states = 2 * groups
    net = state * 2 + yh
    near = ("ylo", "core", "yh")
    gathered = everyone(walkers.reshape(2, 126), near, groups * ny)
    walk = gathered.reshape(groups, ny, 2, 126).transpose(0, 2, 1, 3).reshape(states * ny, 126)
    nuc = jnp.repeat(nuclei.T, 4, axis=1)
    at = yh.reshape(1).astype(jnp.int32)
    mats = (w_query, w_key, w_value, w_attn_out, w_mlp)
    wout = w_out[:, None, :]
    count = states * ny
    total = count * ROWS
    saved = [shape(total, 128)] + [shape(total, D)] * 4 + [shape(total, HEADS * ROWS)] + [shape(total, D)] * 2
    rooms = [pltpu.VMEM(a.shape, jnp.float32) for a in saved]
    la, h2, *kept = local(
        forward_kernel, [shape(count, 128), shape(count, D)], at, (walk, nuc, b_mlp, wout), 61,
        (w_embed,) + mats, saved,
        [pltpu.VMEM((FEAT, D), jnp.float32), pltpu.VMEM((5, D, D), jnp.float32)]
        + rooms
        + [pltpu.SemaphoreType.DMA((6,)), pltpu.SemaphoreType.DMA((14,))],
    )

    feat, x, q, k, v, attn_saved, mix, h1 = kept
    grads = [shape(total, D)] * 3 + [shape(total, 3 * D), shape(total, D)]
    y, dm, dh1, dqkv, dh0 = local(
        backward_kernel, [], at, (b_mlp, wout), 61, (feat, x, q, k, v, attn_saved, h1) + mats, grads,
        [pltpu.VMEM((5, D, D), jnp.float32)]
        + rooms[:6] + rooms[7:]
        + [pltpu.VMEM((total, D), jnp.float32), pltpu.VMEM((total, 3 * D), jnp.float32)]
        + [pltpu.VMEM((total, D), jnp.float32)] * 4
        + [pltpu.SemaphoreType.DMA((32,)), pltpu.SemaphoreType.DMA((8,))],
    )

    logs = everyone(la[:, 0], ("ylo", "core", "x", "yh", "z"), groups * nx * ny * nz)
    logs = logs.reshape(groups, nx, ny, nz, states, ny)
    every = logs.transpose(0, 2, 4, 1, 5, 3).reshape(states, states, walker_count)
    home = jnp.diagonal(every, axis1=0, axis2=1).T
    margins = jnp.mean(jnp.exp(every - home[None]), axis=2).T
    zi = lax.axis_index("z")
    logs = lax.dynamic_index_in_dim(lax.dynamic_index_in_dim(logs, xi, 1, False), zi, 2, False)
    logs = logs.reshape(states, states, ny)
    home = jnp.diagonal(logs, axis1=0, axis2=1).T
    ratios = jnp.exp(logs - home[None])
    identity = jnp.eye(states, dtype=jnp.float32)
    coupling = margins.T * (1.0 - identity)
    denominator = jnp.sum(coupling[:, :, None] * ratios.transpose(1, 0, 2), axis=1) / walker_count
    cot = coupling.T[:, :, None] * ratios / walker_count - identity[:, :, None] * denominator[None]
    own = lax.dynamic_index_in_dim(cot, net, 0, False).reshape(count)
    own = jnp.broadcast_to(own[:, None], (count, 128))

    place = jnp.stack([xi, yh]).astype(jnp.int32)
    sources = (feat, x, mix, y, dm, dh1, dqkv, dh0)
    pieces = local(
        weights_kernel, [shape(BLOCK, D)] * 4, place, (own, h2), 61, sources, (),
        [pltpu.VMEM(a.shape, jnp.float32) for a in sources]
        + [pltpu.VMEM((SPLIT, BLOCK, D), jnp.float32), pltpu.SemaphoreType.DMA((8,))],
    )
    mine = pieces[0]
    for d, piece in zip((2, 1, -1), pieces[1:]):
        mine = mine + shift(piece, "x", d, nx)
    mine = jnp.sum(
        lax.all_to_all(mine.reshape(nz, BLOCK // nz, D), "z", 0, 0, tiled=False), axis=0
    )
    mine = everyone(mine, "z", nz).reshape(BLOCK, D)
    a, c = mine[:HALF], mine[HALF:]
    a_far = shift(a, "yh", 1, ny)
    c_far = [shift(c, "x", d, nx) for d in (2, 1, -1)]
    a_far, *c_far = lax.optimization_barrier((a_far, *c_far))
    a = jnp.stack([a, a_far])
    c = jnp.stack([c, *c_far])
    arrays = [a] + [shift(a, "x", d, nx) for d in (2, 1, -1)] + [c, shift(c, "yh", 1, ny)]
    mat = shape(2, D, D)
    mlp, attn, query, key, value, embed, bias, out = local(
        assemble_kernel, [mat] * 5 + [shape(2, FEAT, D), shape(2, 1, D), shape(2, 1, D)],
        place, arrays, 4,
    )
    return (
        margins, embed, query[:, None], key[:, None], value[:, None],
        attn[:, None], mlp[:, None], bias, out[:, 0],
    )


def solution(mesh):
    fine = Mesh(mesh.devices.reshape(2, 2, 4, 2, 8), ("ylo", "core", "x", "yh", "z"))
    s, w = ("ylo", "core"), ("x", "yh", "z")
    return jax.shard_map(
        shards,
        mesh=fine,
        in_specs=(P(s, w, None), P()) + (P(s),) * 8,
        out_specs=(P(),) + (P(s),) * 8,
        check_vma=False,
    )
```
